256 devices in a mesh: rep: 4 (over x), ep: 64 (over y, z, core).
Axes of the slice: x: 4, y: 4, z: 8, core: 2. Of those that a mesh axis runs over, the one named last changes fastest.
Arguments:
- tokens: bfloat16 [32768, 2048], P(('rep', 'ep')), may hold values from -6 to 6
- expert_ids: int32 [32768, 2], P(('rep', 'ep')), may hold values from 0 to 63, all different within a row; in each aligned block of 128 rows (0 to 127, 128 to 255, ...) at most 5 rows name the same one
- route_weights: bfloat16 [32768, 2], P(('rep', 'ep')), may hold values from 0.099609375 to 1
- w_gate_up: bfloat16 [64, 2048, 1536], P('ep', 'rep'), may hold values from -0.125 to 0.125
- w_down: bfloat16 [64, 2048, 768], P('ep', 'rep'), may hold values from -0.21875 to 0.21875
- grad_out: bfloat16 [32768, 2048], P(('rep', 'ep')), may hold values from -1.5 to 1.5
Outputs:
- mixed: bfloat16 [32768, 2048], P(('rep', 'ep'))
- grad_tokens: bfloat16 [32768, 2048], P(('rep', 'ep'))
- grad_gate_up: bfloat16 [64, 2048, 1536], P('ep', 'rep')
- grad_down: bfloat16 [64, 2048, 768], P('ep', 'rep')
- route_grad: float32 [32768, 2], P(('rep', 'ep'))
The draws below stay inside these ranges and needn't reach their ends.
Inputs may be any that keep to these rules, and one draw needn't show every extreme that they name: `expert_ids`: each token names 2 different experts. Among the rows of one device no expert is named more than 5 times, and in every draw some device names some expert exactly 5 times.
All inputs are finite; a program needn't handle non-finite values.
Results may differ from the reference program's by a relative error of at most 0.0095.
Values may be sent and summed in bfloat16 or wider, within the bound.
A program may use at most 128 MiB of HBM per device.

```python
import math
import jax
import jax.numpy as jnp
import numpy as np
from jax import lax

D = 2048
F = 768
TOPK = 2
TOK_DEV = 128
EXPERTS = 64
TOKENS = 32768
CAP = 5
N_REP = 4


def level_of(stream_key, dims, split, low, top_value):
    def one(position, blocks):
        steps = jax.random.uniform(jax.random.fold_in(jax.random.fold_in(stream_key, 6), position), (blocks,), jnp.float32, low / len(split), top_value / len(split))
        return jnp.repeat(jnp.exp(steps), dims[position] // blocks).reshape((-1,) + (1,) * (len(dims) - position - 1))

    gain = one(*split[0])
    for cut in split[1:]:
        gain = gain * one(*cut)
    return gain


def shared_out(key, own, number, rows, count, top, limit, skew):
    order = jax.random.permutation(key, count)
    crowded, common = portions_of(count, rows * top, limit, skew, True), portions_of(count, rows * top, limit, skew, False)
    places = jnp.arange(count)

    def named(sizes, rotation):
        used = int((sizes > 0).sum())
        fixed = max(1, used // 4)
        shifted = fixed + (places - fixed + rotation * (used - fixed)) % max(1, count - fixed)
        return jnp.zeros((count,), jnp.int32).at[order[jnp.where(places < fixed, places, shifted)]].set(jnp.asarray(sizes, jnp.int32))

    sizes = jnp.where(number % 4 == 0, named(crowded, number // 4), named(common, number - number // 4 - 1))
    mixed = jax.random.permutation(jax.random.fold_in(own, 3), count)
    source_of, sink = mixed[0:count // 2 * 2:2], mixed[1:count // 2 * 2:2]
    room = jnp.minimum(sizes[source_of] - 1, limit - sizes[sink]) // 2
    room = jnp.where((source_of == order[0]) | (sink == order[0]) | (sizes[sink] == 0), 0, jnp.maximum(room, 0))
    shifted = jax.random.randint(jax.random.fold_in(own, 4), (count // 2,), 0, 1 << 20) % (room + 1)
    sizes = sizes.at[source_of].add(-shifted).at[sink].add(shifted)
    members = jnp.searchsorted(jnp.cumsum(sizes), jnp.arange(rows * top), side="right").astype(jnp.int32)
    grid = members.reshape(top, rows).T
    grid = grid[jax.random.permutation(jax.random.fold_in(own, 1), rows)]
    rotation = jax.random.randint(jax.random.fold_in(own, 2), (rows, 1), 0, top)
    return jnp.take_along_axis(grid, (jnp.arange(top)[None, :] + rotation) % top, axis=1)


def portions_of(count, total, bound, skew, full):
    portions = [(1 << 20) // math.isqrt(standing ** skew) + 1 for standing in range(1, count + 1)]
    largest = bound if full else min(bound, max(-(-total // count), total * portions[0] // sum(portions)))
    least = 1 if total - largest >= count - 1 else 0
    given, spare = [largest] + [least] * (count - 1), total - largest - least * (count - 1)
    while spare > 0:
        free = [i for i in range(1, count) if given[i] < largest] or [i for i in range(1, count) if given[i] < bound]
        whole, left = sum([portions[i] for i in free]), spare
        for i in free:
            more = min(bound - given[i], max(1, left * portions[i] // whole), spare)
            given[i] = given[i] + more
            spare = spare - more
    return np.array(given)


def normal_values(stream_key, dims, scale, reach, split=(), held_as=jnp.bfloat16):
    values = jax.random.normal(stream_key, dims, jnp.float32) * scale
    if len(split) > 0:
        values = level_of(stream_key, dims, split, -0.22, 0.18) * values
    return jnp.clip(values, min=-reach, max=reach).astype(held_as)


def setup_inputs(seed: int = 0) -> dict:
    key_of = jax.random.split(jax.random.key(seed), 7)
    tokens = normal_values(key_of[0], (TOKENS, D), 1.0, 6.0, ((0, 256),))
    expert_ids_keys = jax.random.split(jax.random.fold_in(key_of[1], 1), TOKENS // TOK_DEV)
    expert_ids_turns = jax.random.permutation(jax.random.fold_in(key_of[1], 3), TOKENS // TOK_DEV)
    expert_ids = jax.vmap(lambda own, number: shared_out(jax.random.fold_in(key_of[1], 2), own, number, TOK_DEV, EXPERTS, TOPK, CAP, 2))(expert_ids_keys, expert_ids_turns).reshape((TOKENS, TOPK))
    route_weights = jnp.clip(0.099609375 + 0.9003906 * jax.random.uniform(key_of[2], (TOKENS, TOPK), jnp.float32) ** level_of(key_of[2], (TOKENS, TOPK), ((0, 256),), -0.2, 0.2), 0.099609375, 1.0).astype(jnp.bfloat16)
    w_gate_up = normal_values(key_of[3], (EXPERTS, D, 2 * F), D ** -0.5, 0.125, ((0, 64), (1, 4)))
    w_down = normal_values(key_of[4], (EXPERTS, D, F), F ** -0.5, 0.21875, ((0, 64), (1, 4)))
    grad_out = normal_values(key_of[5], (TOKENS, D), 0.25, 1.5, ((0, 256),))
    return {"tokens": tokens, "expert_ids": expert_ids, "route_weights": route_weights, "w_gate_up": w_gate_up, "w_down": w_down, "grad_out": grad_out}


def swiglu_forward(slot_rows, weight_gu, weight_down):
    hidden_size = weight_down.shape[1]
    gate_up = jnp.dot(slot_rows, weight_gu, preferred_element_type=jnp.float32)
    gate_part = gate_up[:, :hidden_size]
    up_part = gate_up[:, hidden_size:]
    activated = (gate_part * jax.nn.sigmoid(gate_part) * up_part).astype(jnp.bfloat16)
    outputs = lax.dot_general(activated, weight_down, (((1,), (1,)), ((), ())), preferred_element_type=jnp.float32).astype(jnp.bfloat16)
    return gate_up, activated, outputs


def swiglu_backward(cotangent, gate_up, weight_gu, weight_down):
    hidden_size = weight_down.shape[1]
    gate_part = gate_up[:, :hidden_size]
    up_part = gate_up[:, hidden_size:]
    grad_hidden = jnp.dot(cotangent, weight_down, preferred_element_type=jnp.float32)
    sigmoid_gate = jax.nn.sigmoid(gate_part)
    slope = sigmoid_gate * (1.0 + gate_part * (1.0 - sigmoid_gate))
    grad_gu = jnp.concatenate([grad_hidden * up_part * slope, grad_hidden * gate_part * sigmoid_gate], axis=1).astype(jnp.bfloat16)
    grad_rows = lax.dot_general(grad_gu, weight_gu, (((1,), (1,)), ((), ())), preferred_element_type=jnp.float32).astype(jnp.bfloat16)
    return grad_gu, grad_rows


def reference(tokens, expert_ids, route_weights, w_gate_up, w_down, grad_out):
    group_slots = 2 * TOK_DEV * TOPK
    assign_total = TOKENS * TOPK
    flat_ids = expert_ids.reshape(-1).astype(jnp.int32)
    one_hot = (flat_ids[:, None] == jnp.arange(EXPERTS, dtype=jnp.int32)[None, :]).astype(jnp.int32)
    running = jnp.cumsum(one_hot.reshape(N_REP, assign_total // N_REP, EXPERTS), axis=1).reshape(assign_total, EXPERTS)
    rank = jnp.sum(running * one_hot, axis=1) - 1
    group_of = jnp.arange(assign_total, dtype=jnp.int32) // (assign_total // N_REP)
    target = flat_ids * (N_REP * group_slots) + group_of * group_slots + rank
    table = jnp.full((EXPERTS * N_REP * group_slots,), assign_total, jnp.int32)
    table = table.at[target].set(jnp.arange(assign_total, dtype=jnp.int32)).reshape(EXPERTS, N_REP * group_slots)
    tokens_ext = jnp.concatenate([tokens, jnp.zeros((1, D), jnp.bfloat16)], axis=0)
    grad_ext = jnp.concatenate([grad_out, jnp.zeros((1, D), jnp.bfloat16)], axis=0)
    weight_ext = jnp.concatenate([route_weights.reshape(-1), jnp.zeros((1,), jnp.bfloat16)], axis=0)

    def per_expert(carry, inputs):
        out_assign, rows_assign = carry
        index_row, weight_gu, weight_down = inputs
        token_row = index_row // TOPK
        slot_rows = tokens_ext[token_row]
        cotangent = (weight_ext[index_row].astype(jnp.float32)[:, None] * grad_ext[token_row].astype(jnp.float32)).astype(jnp.bfloat16)
        gate_up, activated, outputs = swiglu_forward(slot_rows, weight_gu, weight_down)
        grad_gu, grad_rows = swiglu_backward(cotangent, gate_up, weight_gu, weight_down)
        out_assign = out_assign.at[index_row].set(outputs)
        rows_assign = rows_assign.at[index_row].set(grad_rows)
        part_gu = jnp.einsum("rsd,rsf->rdf", slot_rows.reshape(N_REP, group_slots, D).astype(jnp.float32), grad_gu.reshape(N_REP, group_slots, 2 * F).astype(jnp.float32))
        part_gu = lax.optimization_barrier(part_gu.astype(jnp.bfloat16))
        sum_gu = jnp.sum(part_gu.astype(jnp.float32), axis=0).astype(jnp.bfloat16)
        part_down = jnp.einsum("rsd,rsf->rdf", cotangent.reshape(N_REP, group_slots, D).astype(jnp.float32), activated.reshape(N_REP, group_slots, F).astype(jnp.float32))
        part_down = lax.optimization_barrier(part_down.astype(jnp.bfloat16))
        sum_down = jnp.sum(part_down.astype(jnp.float32), axis=0).astype(jnp.bfloat16)
        return (out_assign, rows_assign), (sum_gu, sum_down)

    initial = (jnp.zeros((assign_total + 1, D), jnp.bfloat16), jnp.zeros((assign_total + 1, D), jnp.bfloat16))
    (out_assign, rows_assign), (grad_gate_up, grad_down) = lax.scan(per_expert, initial, (table, w_gate_up, w_down))
    expert_out = out_assign[:assign_total].reshape(TOKENS, TOPK, D).astype(jnp.float32)
    mixed = jnp.sum(route_weights.astype(jnp.float32)[:, :, None] * expert_out, axis=1).astype(jnp.bfloat16)
    route_grad = jnp.sum(grad_out.astype(jnp.float32)[:, None, :] * expert_out, axis=2)
    grad_tokens = jnp.sum(rows_assign[:assign_total].reshape(TOKENS, TOPK, D).astype(jnp.float32), axis=1).astype(jnp.bfloat16)
    return mixed, grad_tokens, grad_gate_up, grad_down, route_grad
```

```python
import functools

import jax
import jax.numpy as jnp
from jax import lax
from jax.experimental import pallas as pl
from jax.experimental.pallas import tpu as pltpu
from jax.sharding import PartitionSpec as P

MESH = pl.DeviceIdType.MESH
F32 = jnp.float32
BF16 = jnp.bfloat16
LANES = 128


def layer_kernel(
    sizes,
    source_ref,
    slot_weight_ref,
    target_ref,
    pair_weight_ref,
    tokens_ref,
    grad_ref,
    wg_hbm,
    wd_hbm,
    mixed_ref,
    gtok_ref,
    ggu_ref,
    gdn_ref,
    rg_ref,
    wg,
    wd,
    own_g,
    own_d,
    part_g,
    part_d,
    rin_g,
    rin_d,
    din_g,
    din_d,
    send_x,
    recv_x,
    send_c,
    recv_c,
    send_o,
    recv_o,
    send_r,
    recv_r,
    x2,
    c2,
    scr,
    acc,
    gh,
    hid,
    ggu,
    tok_t,
    grd_t,
    rg_a,
    rg_b,
    local_sem,
    ag_send,
    ag_recv,
    rl_send,
    rl_recv,
    ro_send,
    ro_recv,
    rs_send,
    rs_recv,
    a2a_send,
    a2a_recv,
):
    n_rep, n_ep, cap, tok, width, hidden = sizes
    quarter = width // n_rep
    half = quarter // 2
    tiles = width // LANES
    per_q = quarter // LANES
    slots = n_ep * cap
    x = lax.axis_index("rep")
    e = lax.axis_index("ep")
    right = lax.rem(x + 1, n_rep)
    left = lax.rem(x + n_rep - 1, n_rep)
    quarters = (x, left, right, lax.rem(x + 2, n_rep))

    barrier = pltpu.get_barrier_semaphore()
    for side in (left, right):
        pl.semaphore_signal(barrier, inc=1, device_id=(side, e), device_id_type=MESH)

    @pl.loop(1, n_ep)
    def _(i):
        pl.semaphore_signal(
            barrier, inc=1, device_id=(x, lax.rem(e + i, n_ep)), device_id_type=MESH
        )

    local = [
        pltpu.make_async_copy(wg_hbm, wg.at[0], local_sem.at[0]),
        pltpu.make_async_copy(wd_hbm, wd.at[0], local_sem.at[1]),
    ]
    for copy in local:
        copy.start()

    hbm = (wg_hbm, wd_hbm)
    full = (wg, wd)
    part = (part_g, part_d)
    rin = (rin_g, rin_d)
    din = (din_g, din_d)
    own = (own_g, own_d)
    halves = (pl.ds(0, half), pl.ds(half, half))
    sides = (right, left)

    def gather_copy(k, d, h):
        return pltpu.make_async_remote_copy(
            src_ref=hbm[k].at[halves[h], :],
            dst_ref=full[k].at[1 + d, halves[h], :],
            send_sem=ag_send.at[k, d, h],
            recv_sem=ag_recv.at[k, d, h],
            device_id=(sides[d], e),
            device_id_type=MESH,
        )

    def relay_copy(k, d):
        return pltpu.make_async_remote_copy(
            src_ref=full[k].at[1 + d, halves[d], :],
            dst_ref=full[k].at[3, halves[d], :],
            send_sem=rl_send.at[k, d],
            recv_sem=rl_recv.at[k, d],
            device_id=(sides[d], e),
            device_id_type=MESH,
        )

    def far_copy(k, d):
        return pltpu.make_async_remote_copy(
            src_ref=part[k].at[2, halves[d], :],
            dst_ref=rin[k].at[d],
            send_sem=ro_send.at[k, d],
            recv_sem=ro_recv.at[k, d],
            device_id=(sides[d], e),
            device_id_type=MESH,
        )

    def near_copy(k, d, h):
        return pltpu.make_async_remote_copy(
            src_ref=part[k].at[1 - d, halves[h], :],
            dst_ref=din[k].at[d, halves[h], :],
            send_sem=rs_send.at[k, d, h],
            recv_sem=rs_recv.at[k, d, h],
            device_id=(sides[d], e),
            device_id_type=MESH,
        )

    def send_all(send, recv, n):
        @pl.loop(1, n_ep)
        def _(i):
            peer = lax.rem(e + i, n_ep)
            pltpu.make_async_remote_copy(
                src_ref=send.at[pl.ds(peer * cap, cap)],
                dst_ref=recv.at[pl.ds(e * cap, cap)],
                send_sem=a2a_send.at[n],
                recv_sem=a2a_recv.at[n],
                device_id=(x, peer),
                device_id_type=MESH,
            ).start()

        mine = pl.ds(e * cap, cap)
        recv[mine] = send[mine]

    def wait_all(buf, sem):
        rest = buf.at[pl.ds(0, (n_ep - 1) * cap)]
        pltpu.make_async_copy(rest, rest, sem).wait()

    def tiled(src, dst):
        for s in range(n_rep):
            for j in range(per_q):
                col = pl.multiple_of(quarters[s] * quarter + j * LANES, LANES)
                scr[pl.ds(s * per_q + j, tok, stride=tiles), :] = src[:, pl.ds(col, LANES)].astype(F32)

        @pl.loop(0, tok // 8)
        def _(i):
            rows = pl.ds(pl.multiple_of(i * 8 * tiles, 16), 8 * tiles)
            dst[pl.ds(i * 8, 8)] = scr[rows, :].astype(BF16).reshape(8, tiles, LANES)

        dst[tok] = jnp.zeros((tiles, LANES), BF16)

    def row(r):
        return pl.ds(pl.multiple_of(r * tiles, 16), tiles)

    tiled(tokens_ref, tok_t)

    @pl.loop(0, slots // 8)
    def _(i):
        for j in range(8):
            s = i * 8 + j
            send_x[s] = tok_t[source_ref[s]]

    pl.semaphore_wait(barrier, n_ep + 1)
    for k in range(2):
        for h in range(2):
            for d in range(2):
                gather_copy(k, d, h ^ d).start()
    send_all(send_x, recv_x, 0)

    tiled(grad_ref, grd_t)

    @pl.loop(0, slots // 8)
    def _(i):
        for j in range(8):
            s = i * 8 + j
            rows = grd_t[source_ref[s]].astype(F32) * slot_weight_ref[s]
            send_c[s] = rows.astype(BF16)

    send_all(send_c, recv_c, 1)

    def spread(recv, dst):
        @pl.loop(0, slots // 8)
        def _(i):
            rows = pl.ds(pl.multiple_of(i * 8 * tiles, 16), 8 * tiles)
            scr[rows, :] = recv[pl.ds(i * 8, 8)].astype(F32).reshape(8 * tiles, LANES)

        for s in range(n_rep):
            for j in range(per_q):
                dst[s, :, j * LANES : (j + 1) * LANES] = scr[
                    pl.ds(s * per_q + j, slots, stride=tiles), :
                ].astype(BF16)

    def product(s, lhs, rhs, out, columns, step, first):
        @pl.loop(0, columns // step)
        def _(n):
            cols = pl.ds(pl.multiple_of(n * step, LANES), step)
            y = jnp.dot(lhs[s], rhs[s, :, cols], preferred_element_type=F32)
            if first:
                out[:, cols] = y
            else:
                out[:, cols] = out[:, cols] + y

    def returned(lhs, rhs, send, n_blocks):
        for s in range(n_rep):
            for j in range(per_q):
                scr[pl.ds(s * per_q + j, slots, stride=tiles), :] = lax.dot_general(
                    lhs[...],
                    rhs[s, j * LANES : (j + 1) * LANES, :],
                    (((1,), (1,)), ((), ())),
                    preferred_element_type=F32,
                )

        @pl.loop(0, slots // 8)
        def _(i):
            rows = pl.ds(pl.multiple_of(i * 8 * tiles, 16), 8 * tiles)
            send[pl.ds(i * 8, 8)] = scr[rows, :].astype(BF16).reshape(8, tiles, LANES)

    def outer(lhs, rhs, s, h, k, columns, step):
        block = lhs[s, :, h * half : (h + 1) * half]

        @pl.loop(0, columns // step)
        def _(n):
            cols = pl.ds(pl.multiple_of(n * step, LANES), step)
            y = lax.dot_general(
                block, rhs[:, cols], (((0,), (0,)), ((), ())), preferred_element_type=F32
            )
            if s == 0:
                own[k][halves[h], cols] = y
            else:
                part[k][s - 1, halves[h], cols] = y.astype(BF16)

    def partial_grads(lhs, rhs, k, columns, step):
        for d in range(2):
            outer(lhs, rhs, 3, d, k, columns, step)
            far_copy(k, d).start()
        for d in range(2):
            outer(lhs, rhs, 2 - d, 1 - d, k, columns, step)
            near_copy(k, d, 1 - d).start()
        for d in range(2):
            outer(lhs, rhs, 2 - d, d, k, columns, step)

    def pass_on(k):
        for d in range(2):
            far_copy(k, d).wait_recv()

            @pl.loop(0, half // 16)
            def _(i):
                here = pl.ds(pl.multiple_of(i * 16, 16), 16)
                there = pl.ds(pl.multiple_of(d * half + i * 16, 16), 16)
                total = part[k][1 - d, there, :].astype(F32) + rin[k][d, here, :].astype(F32)
                part[k][1 - d, there, :] = total.astype(BF16)

            near_copy(k, d, d).start()

    def finish(k, out):
        for h in range(2):
            for d in range(2):
                near_copy(k, d, h).wait_recv()

            @pl.loop(0, half // 16)
            def _(i):
                rows = pl.ds(pl.multiple_of(h * half + i * 16, 16), 16)
                total = own[k][rows, :] + din[k][0, rows, :].astype(F32) + din[k][1, rows, :].astype(F32)
                out[rows, :] = total.astype(BF16)

    wait_all(recv_x, a2a_recv.at[0])
    spread(recv_x, x2)
    local[0].wait()
    product(0, x2, wg, acc, 2 * hidden, 256, True)
    for d in range(2):
        gather_copy(0, d, d).wait_recv()
        relay_copy(0, d).start()
    for d in range(2):
        gather_copy(0, d, 1 - d).wait_recv()
        product(1 + d, x2, wg, acc, 2 * hidden, 256, False)
    for d in range(2):
        gather_copy(1, d, d).wait_recv()
        relay_copy(1, d).start()
    wait_all(recv_c, a2a_recv.at[1])
    spread(recv_c, c2)
    local[1].wait()
    product(0, c2, wd, gh, hidden, 256, True)
    for d in range(2):
        gather_copy(1, d, 1 - d).wait_recv()
        product(1 + d, c2, wd, gh, hidden, 256, False)
    for d in range(2):
        relay_copy(0, d).wait_recv()
    product(3, x2, wg, acc, 2 * hidden, 256, False)

    @pl.loop(0, slots // 16)
    def _(i):
        rows = pl.ds(pl.multiple_of(i * 16, 16), 16)
        gate = acc[rows, :hidden]
        up = acc[rows, hidden:]
        hid[rows, :] = (gate * jax.nn.sigmoid(gate) * up).astype(BF16)

    partial_grads(c2, hid, 1, hidden, 256)
    for d in range(2):
        relay_copy(1, d).wait_recv()
    product(3, c2, wd, gh, hidden, 256, False)

    @pl.loop(0, slots // 16)
    def _(i):
        rows = pl.ds(pl.multiple_of(i * 16, 16), 16)
        gate = acc[rows, :hidden]
        up = acc[rows, hidden:]
        grad = gh[rows, :]
        s = jax.nn.sigmoid(gate)
        ggu[rows, :hidden] = (grad * up * (s * (1.0 + gate * (1.0 - s)))).astype(BF16)
        ggu[rows, hidden:] = (grad * gate * s).astype(BF16)

    returned(hid, wd, send_o, 0)
    send_all(send_o, recv_o, 2)
    pass_on(1)
    partial_grads(x2, ggu, 0, 2 * hidden, 256)
    returned(ggu, wg, send_r, 0)
    send_all(send_r, recv_r, 3)
    for h in range(2):
        outer(c2, hid, 0, h, 1, hidden, 256)
    for h in range(2):
        outer(x2, ggu, 0, h, 0, 2 * hidden, 256)
    pass_on(0)
    finish(1, gdn_ref)

    def untiled(out):
        for s in range(n_rep):
            for j in range(per_q):
                col = pl.multiple_of(quarters[s] * quarter + j * LANES, LANES)
                out[:, pl.ds(col, LANES)] = scr[pl.ds(s * per_q + j, tok, stride=tiles), :].astype(BF16)

    wait_all(recv_o, a2a_recv.at[2])

    @pl.loop(0, tok // 4)
    def _(i):
        for j in range(4):
            t = i * 4 + j
            first = recv_o[target_ref[2 * t]].astype(F32)
            second = recv_o[target_ref[2 * t + 1]].astype(F32)
            grad = grd_t[t].astype(F32)
            scr[row(t), :] = pair_weight_ref[2 * t] * first + pair_weight_ref[2 * t + 1] * second
            rg_a[pl.ds(t, 1), :] = jnp.sum(grad * first, axis=0, keepdims=True)
            rg_b[pl.ds(t, 1), :] = jnp.sum(grad * second, axis=0, keepdims=True)

    untiled(mixed_ref)
    rg_ref[:, 0:1] = jnp.sum(rg_a[...], axis=1, keepdims=True)
    rg_ref[:, 1:2] = jnp.sum(rg_b[...], axis=1, keepdims=True)

    wait_all(recv_r, a2a_recv.at[3])

    @pl.loop(0, tok // 4)
    def _(i):
        for j in range(4):
            t = i * 4 + j
            first = recv_r[target_ref[2 * t]].astype(F32)
            second = recv_r[target_ref[2 * t + 1]].astype(F32)
            scr[row(t), :] = first + second

    untiled(gtok_ref)
    finish(0, ggu_ref)

    for n, buf in enumerate((send_x, send_c, send_o, send_r)):
        wait_all(buf, a2a_send.at[n])
    for k in range(2):
        for d in range(2):
            relay_copy(k, d).wait_send()
            far_copy(k, d).wait_send()
            for h in range(2):
                gather_copy(k, d, h).wait_send()
                near_copy(k, d, h).wait_send()


def routing(expert_ids, route_weights, n_ep, cap):
    assign = expert_ids.size
    flat = expert_ids.reshape(-1)
    order = jnp.arange(assign, dtype=jnp.int32)
    earlier = (flat[:, None] == flat[None, :]) & (order[None, :] < order[:, None])
    target = flat * cap + jnp.sum(earlier.astype(jnp.int32), axis=1)
    slot = jnp.arange(n_ep * cap, dtype=jnp.int32)
    match = slot[:, None] == target[None, :]
    top = expert_ids.shape[1]
    found = jnp.where(match, (order // top)[None, :] - expert_ids.shape[0], 0)
    source = jnp.sum(found, axis=1) + expert_ids.shape[0]
    weights = route_weights.reshape(-1).astype(F32)
    slot_weight = jnp.sum(jnp.where(match, weights[None, :], 0.0), axis=1)
    return source, slot_weight, target, weights


def per_device(n_rep, n_ep, tokens, expert_ids, route_weights, w_gate_up, w_down, grad_out):
    tok, width = tokens.shape
    top = expert_ids.shape[1]
    hidden = w_down.shape[2]
    cap = 5 * tok * top // (4 * n_ep)
    slots = n_ep * cap
    quarter = width // n_rep
    half = quarter // 2
    tiles = width // LANES
    source, slot_weight, target, weights = routing(expert_ids, route_weights, n_ep, cap)
    smem = pl.BlockSpec(memory_space=pltpu.SMEM)
    vmem = pl.BlockSpec(memory_space=pltpu.VMEM)
    anywhere = pl.BlockSpec(memory_space=pl.ANY)
    V = pltpu.VMEM
    rows = V((slots, tiles, LANES), BF16)
    dma = pltpu.SemaphoreType.DMA
    mixed, gtok, ggu, gdn, rg = pl.pallas_call(
        functools.partial(layer_kernel, (n_rep, n_ep, cap, tok, width, hidden)),
        out_shape=(
            jax.ShapeDtypeStruct((tok, width), BF16),
            jax.ShapeDtypeStruct((tok, width), BF16),
            jax.ShapeDtypeStruct((quarter, 2 * hidden), BF16),
            jax.ShapeDtypeStruct((quarter, hidden), BF16),
            jax.ShapeDtypeStruct((tok, top), F32),
        ),
        in_specs=[smem] * 4 + [vmem] * 2 + [anywhere] * 2,
        out_specs=[vmem] * 5,
        scratch_shapes=[
            V((n_rep, quarter, 2 * hidden), BF16),
            V((n_rep, quarter, hidden), BF16),
            V((quarter, 2 * hidden), F32),
            V((quarter, hidden), F32),
            V((n_rep - 1, quarter, 2 * hidden), BF16),
            V((n_rep - 1, quarter, hidden), BF16),
            V((2, half, 2 * hidden), BF16),
            V((2, half, hidden), BF16),
            V((2, quarter, 2 * hidden), BF16),
            V((2, quarter, hidden), BF16),
        ]
        + [rows] * 8
        + [
            V((n_rep, slots, quarter), BF16),
            V((n_rep, slots, quarter), BF16),
            V((slots * tiles, LANES), F32),
            V((slots, 2 * hidden), F32),
            V((slots, hidden), F32),
            V((slots, hidden), BF16),
            V((slots, 2 * hidden), BF16),
            V((tok + 1, tiles, LANES), BF16),
            V((tok + 1, tiles, LANES), BF16),
            V((tok, LANES), F32),
            V((tok, LANES), F32),
            dma((2,)),
            dma((2, 2, 2)),
            dma((2, 2, 2)),
            dma((2, 2)),
            dma((2, 2)),
            dma((2, 2)),
            dma((2, 2)),
            dma((2, 2, 2)),
            dma((2, 2, 2)),
            dma((4,)),
            dma((4,)),
        ],
        compiler_params=pltpu.CompilerParams(
            collective_id=0, has_side_effects=True, vmem_limit_bytes=67043328
        ),
    )(source, slot_weight, target, weights, tokens, grad_out, w_gate_up[0], w_down[0])
    return mixed, gtok, ggu[None], gdn[None], rg


def solution(mesh):
    both = ("rep", "ep")
    split = P(both, None)
    weights = P("ep", "rep", None)
    return jax.shard_map(
        functools.partial(per_device, mesh.shape["rep"], mesh.shape["ep"]),
        mesh=mesh,
        in_specs=(split, split, split, weights, weights, split),
        out_specs=(split, split, weights, weights, split),
        check_vma=False,
    )
```

```python
import functools

import jax
import jax.numpy as jnp
from jax import lax
from jax.experimental import pallas as pl
from jax.experimental.pallas import tpu as pltpu
from jax.sharding import PartitionSpec as P

MESH = pl.DeviceIdType.MESH
F32 = jnp.float32
BF16 = jnp.bfloat16
LANES = 128


def layer_kernel(
    sizes,
    ids_ref,
    pair_ref,
    tokens_ref,
    grad_ref,
    wg_hbm,
    wd_hbm,
    mixed_ref,
    gtok_ref,
    ggu_ref,
    gdn_ref,
    rg_ref,
    wg,
    wd,
    own_g,
    own_d,
    part_g,
    part_d,
    rin_g,
    rin_d,
    din_g,
    din_d,
    send_x,
    recv_x,
    send_c,
    recv_c,
    send_o,
    recv_o,
    send_r,
    recv_r,
    x2,
    c2,
    scr,
    acc,
    gh,
    hid,
    ggu,
    tok_t,
    grd_t,
    rg_a,
    rg_b,
    index_v,
    weight_v,
    index_s,
    weight_s,
    local_sem,
    ag_send,
    ag_recv,
    rl_send,
    rl_recv,
    ro_send,
    ro_recv,
    rs_send,
    rs_recv,
    a2a_send,
    a2a_recv,
):
    n_rep, n_ep, cap, tok, width, hidden = sizes
    quarter = width // n_rep
    half = quarter // 2
    tiles = width // LANES
    per_q = quarter // LANES
    slots = n_ep * cap
    x = lax.axis_index("rep")
    e = lax.axis_index("ep")
    right = lax.rem(x + 1, n_rep)
    left = lax.rem(x + n_rep - 1, n_rep)
    quarters = (x, left, right, lax.rem(x + 2, n_rep))

    barrier = pltpu.get_barrier_semaphore()
    for side in (left, right):
        pl.semaphore_signal(barrier, inc=1, device_id=(side, e), device_id_type=MESH)

    @pl.loop(1, n_ep)
    def _(i):
        pl.semaphore_signal(
            barrier, inc=1, device_id=(x, lax.rem(e + i, n_ep)), device_id_type=MESH
        )

    local = [
        pltpu.make_async_copy(wg_hbm, wg.at[0], local_sem.at[0]),
        pltpu.make_async_copy(wd_hbm, wd.at[0], local_sem.at[1]),
    ]
    for copy in local:
        copy.start()

    hbm = (wg_hbm, wd_hbm)
    full = (wg, wd)
    part = (part_g, part_d)
    rin = (rin_g, rin_d)
    din = (din_g, din_d)
    own = (own_g, own_d)
    halves = (pl.ds(0, half), pl.ds(half, half))
    sides = (right, left)

    def gather_copy(k, d, h):
        return pltpu.make_async_remote_copy(
            src_ref=hbm[k].at[halves[h], :],
            dst_ref=full[k].at[1 + d, halves[h], :],
            send_sem=ag_send.at[k, d, h],
            recv_sem=ag_recv.at[k, d, h],
            device_id=(sides[d], e),
            device_id_type=MESH,
        )

    def relay_copy(k, d):
        return pltpu.make_async_remote_copy(
            src_ref=full[k].at[1 + d, halves[d], :],
            dst_ref=full[k].at[3, halves[d], :],
            send_sem=rl_send.at[k, d],
            recv_sem=rl_recv.at[k, d],
            device_id=(sides[d], e),
            device_id_type=MESH,
        )

    def far_copy(k, d):
        return pltpu.make_async_remote_copy(
            src_ref=part[k].at[2, halves[d], :],
            dst_ref=rin[k].at[d],
            send_sem=ro_send.at[k, d],
            recv_sem=ro_recv.at[k, d],
            device_id=(sides[d], e),
            device_id_type=MESH,
        )

    def near_copy(k, d, h):
        return pltpu.make_async_remote_copy(
            src_ref=part[k].at[1 - d, halves[h], :],
            dst_ref=din[k].at[d, halves[h], :],
            send_sem=rs_send.at[k, d, h],
            recv_sem=rs_recv.at[k, d, h],
            device_id=(sides[d], e),
            device_id_type=MESH,
        )

    def send_all(send, recv, n):
        @pl.loop(1, n_ep)
        def _(i):
            peer = lax.rem(e + i, n_ep)
            pltpu.make_async_remote_copy(
                src_ref=send.at[pl.ds(peer * cap, cap)],
                dst_ref=recv.at[pl.ds(e * cap, cap)],
                send_sem=a2a_send.at[n],
                recv_sem=a2a_recv.at[n],
                device_id=(x, peer),
                device_id_type=MESH,
            ).start()

        mine = pl.ds(e * cap, cap)
        recv[mine] = send[mine]

    def wait_all(buf, sem):
        rest = buf.at[pl.ds(0, (n_ep - 1) * cap)]
        pltpu.make_async_copy(rest, rest, sem).wait()

    def tiled(src, dst):
        for s in range(n_rep):
            for j in range(per_q):
                col = pl.multiple_of(quarters[s] * quarter + j * LANES, LANES)
                scr[pl.ds(s * per_q + j, tok, stride=tiles), :] = src[:, pl.ds(col, LANES)].astype(F32)

        @pl.loop(0, tok // 8)
        def _(i):
            rows = pl.ds(pl.multiple_of(i * 8 * tiles, 16), 8 * tiles)
            dst[pl.ds(i * 8, 8)] = scr[rows, :].astype(BF16).reshape(8, tiles, LANES)

        dst[tok] = jnp.zeros((tiles, LANES), BF16)

    def row(r):
        return pl.ds(pl.multiple_of(r * tiles, 16), tiles)

    tables = [
        pltpu.make_async_copy(index_v, index_s, local_sem.at[2]),
        pltpu.make_async_copy(weight_v, weight_s, local_sem.at[3]),
    ]
    routing(ids_ref, pair_ref, index_v, weight_v, cap)
    for copy in tables:
        copy.start()
    tiled(tokens_ref, tok_t)
    for copy in tables:
        copy.wait()

    @pl.loop(0, slots // 8)
    def _(i):
        for j in range(8):
            s = i * 8 + j
            send_x[s] = tok_t[index_s[0, s]]

    pl.semaphore_wait(barrier, n_ep + 1)
    for k in range(2):
        for h in range(2):
            for d in range(2):
                gather_copy(k, d, h ^ d).start()
    send_all(send_x, recv_x, 0)

    tiled(grad_ref, grd_t)

    @pl.loop(0, slots // 8)
    def _(i):
        for j in range(8):
            s = i * 8 + j
            rows = grd_t[index_s[0, s]].astype(F32) * weight_s[0, s]
            send_c[s] = rows.astype(BF16)

    send_all(send_c, recv_c, 1)

    def spread(recv, dst):
        @pl.loop(0, slots // 8)
        def _(i):
            rows = pl.ds(pl.multiple_of(i * 8 * tiles, 16), 8 * tiles)
            scr[rows, :] = recv[pl.ds(i * 8, 8)].astype(F32).reshape(8 * tiles, LANES)

        for s in range(n_rep):
            for j in range(per_q):
                dst[s, :, j * LANES : (j + 1) * LANES] = scr[
                    pl.ds(s * per_q + j, slots, stride=tiles), :
                ].astype(BF16)

    def product(s, lhs, rhs, out, columns, step, first):
        @pl.loop(0, columns // step)
        def _(n):
            cols = pl.ds(pl.multiple_of(n * step, LANES), step)
            y = jnp.dot(lhs[s], rhs[s, :, cols], preferred_element_type=F32)
            if first:
                out[:, cols] = y
            else:
                out[:, cols] = out[:, cols] + y

    def returned(lhs, rhs, send, n_blocks):
        for s in range(n_rep):
            for j in range(per_q):
                scr[pl.ds(s * per_q + j, slots, stride=tiles), :] = lax.dot_general(
                    lhs[...],
                    rhs[s, j * LANES : (j + 1) * LANES, :],
                    (((1,), (1,)), ((), ())),
                    preferred_element_type=F32,
                )

        @pl.loop(0, slots // 8)
        def _(i):
            rows = pl.ds(pl.multiple_of(i * 8 * tiles, 16), 8 * tiles)
            send[pl.ds(i * 8, 8)] = scr[rows, :].astype(BF16).reshape(8, tiles, LANES)

    def outer(lhs, rhs, s, h, k, columns, step):
        block = lhs[s, :, h * half : (h + 1) * half]

        @pl.loop(0, columns // step)
        def _(n):
            cols = pl.ds(pl.multiple_of(n * step, LANES), step)
            y = lax.dot_general(
                block, rhs[:, cols], (((0,), (0,)), ((), ())), preferred_element_type=F32
            )
            if s == 0:
                own[k][halves[h], cols] = y
            else:
                part[k][s - 1, halves[h], cols] = y.astype(BF16)

    def partial_grads(lhs, rhs, k, columns, step):
        for d in range(2):
            outer(lhs, rhs, 3, d, k, columns, step)
            far_copy(k, d).start()
        for d in range(2):
            outer(lhs, rhs, 2 - d, 1 - d, k, columns, step)
            near_copy(k, d, 1 - d).start()
        for d in range(2):
            outer(lhs, rhs, 2 - d, d, k, columns, step)

    def pass_on(k):
        for d in range(2):
            far_copy(k, d).wait_recv()

            @pl.loop(0, half // 16)
            def _(i):
                here = pl.ds(pl.multiple_of(i * 16, 16), 16)
                there = pl.ds(pl.multiple_of(d * half + i * 16, 16), 16)
                total = part[k][1 - d, there, :].astype(F32) + rin[k][d, here, :].astype(F32)
                part[k][1 - d, there, :] = total.astype(BF16)

            near_copy(k, d, d).start()

    def finish(k, out):
        for h in range(2):
            for d in range(2):
                near_copy(k, d, h).wait_recv()

            @pl.loop(0, half // 16)
            def _(i):
                rows = pl.ds(pl.multiple_of(h * half + i * 16, 16), 16)
                total = own[k][rows, :] + din[k][0, rows, :].astype(F32) + din[k][1, rows, :].astype(F32)
                out[rows, :] = total.astype(BF16)

    wait_all(recv_x, a2a_recv.at[0])
    spread(recv_x, x2)
    local[0].wait()
    product(0, x2, wg, acc, 2 * hidden, 256, True)
    for d in range(2):
        gather_copy(0, d, d).wait_recv()
        relay_copy(0, d).start()
    for d in range(2):
        gather_copy(0, d, 1 - d).wait_recv()
        product(1 + d, x2, wg, acc, 2 * hidden, 256, False)
    for d in range(2):
        gather_copy(1, d, d).wait_recv()
        relay_copy(1, d).start()
    wait_all(recv_c, a2a_recv.at[1])
    spread(recv_c, c2)
    local[1].wait()
    product(0, c2, wd, gh, hidden, 256, True)
    for d in range(2):
        gather_copy(1, d, 1 - d).wait_recv()
        product(1 + d, c2, wd, gh, hidden, 256, False)
    for d in range(2):
        relay_copy(0, d).wait_recv()
    product(3, x2, wg, acc, 2 * hidden, 256, False)

    @pl.loop(0, slots // 16)
    def _(i):
        rows = pl.ds(pl.multiple_of(i * 16, 16), 16)
        gate = acc[rows, :hidden]
        up = acc[rows, hidden:]
        hid[rows, :] = (gate * jax.nn.sigmoid(gate) * up).astype(BF16)

    partial_grads(c2, hid, 1, hidden, 256)
    for d in range(2):
        relay_copy(1, d).wait_recv()
    product(3, c2, wd, gh, hidden, 256, False)

    @pl.loop(0, slots // 16)
    def _(i):
        rows = pl.ds(pl.multiple_of(i * 16, 16), 16)
        gate = acc[rows, :hidden]
        up = acc[rows, hidden:]
        grad = gh[rows, :]
        s = jax.nn.sigmoid(gate)
        ggu[rows, :hidden] = (grad * up * (s * (1.0 + gate * (1.0 - s)))).astype(BF16)
        ggu[rows, hidden:] = (grad * gate * s).astype(BF16)

    returned(hid, wd, send_o, 0)
    send_all(send_o, recv_o, 2)
    pass_on(1)
    partial_grads(x2, ggu, 0, 2 * hidden, 256)
    returned(ggu, wg, send_r, 0)
    send_all(send_r, recv_r, 3)
    for h in range(2):
        outer(c2, hid, 0, h, 1, hidden, 256)
    for h in range(2):
        outer(x2, ggu, 0, h, 0, 2 * hidden, 256)
    pass_on(0)
    finish(1, gdn_ref)

    def untiled(out):
        for s in range(n_rep):
            for j in range(per_q):
                col = pl.multiple_of(quarters[s] * quarter + j * LANES, LANES)
                out[:, pl.ds(col, LANES)] = scr[pl.ds(s * per_q + j, tok, stride=tiles), :].astype(BF16)

    wait_all(recv_o, a2a_recv.at[2])

    @pl.loop(0, tok // 4)
    def _(i):
        for j in range(4):
            t = i * 4 + j
            first = recv_o[index_s[1, t]].astype(F32)
            second = recv_o[index_s[2, t]].astype(F32)
            grad = grd_t[t].astype(F32)
            scr[row(t), :] = weight_s[1, t] * first + weight_s[2, t] * second
            rg_a[pl.ds(t, 1), :] = jnp.sum(grad * first, axis=0, keepdims=True)
            rg_b[pl.ds(t, 1), :] = jnp.sum(grad * second, axis=0, keepdims=True)

    untiled(mixed_ref)
    rg_ref[0:1, :] = jnp.sum(rg_a[...].T, axis=0, keepdims=True)
    rg_ref[1:2, :] = jnp.sum(rg_b[...].T, axis=0, keepdims=True)

    wait_all(recv_r, a2a_recv.at[3])

    @pl.loop(0, tok // 4)
    def _(i):
        for j in range(4):
            t = i * 4 + j
            first = recv_r[index_s[1, t]].astype(F32)
            second = recv_r[index_s[2, t]].astype(F32)
            scr[row(t), :] = first + second

    untiled(gtok_ref)
    finish(0, ggu_ref)

    for n, buf in enumerate((send_x, send_c, send_o, send_r)):
        wait_all(buf, a2a_send.at[n])
    for k in range(2):
        for d in range(2):
            relay_copy(k, d).wait_send()
            far_copy(k, d).wait_send()
            for h in range(2):
                gather_copy(k, d, h).wait_send()
                near_copy(k, d, h).wait_send()


def routing(ids_ref, pair_ref, index_v, weight_v, cap):
    top, tok = ids_ref.shape
    slots = index_v.shape[1]
    here = lax.broadcasted_iota(jnp.int32, (tok, tok), 0)
    there = lax.broadcasted_iota(jnp.int32, (tok, tok), 1)
    rows = [jnp.broadcast_to(ids_ref[k : k + 1, :], (tok, tok)) for k in range(top)]
    columns = [r.T for r in rows]
    slot = lax.broadcasted_iota(jnp.int32, (tok, slots), 1)
    token = lax.broadcasted_iota(jnp.int32, (tok, slots), 0)
    source = jnp.full((1, slots), tok, jnp.int32)
    weight = jnp.zeros((1, slots), F32)
    for k in range(top):
        rank = jnp.sum(
            jnp.where((columns[k] == rows[k]) & (here < there), 1, 0), axis=0, keepdims=True
        )
        for m in range(k):
            rank = rank + jnp.sum(jnp.where(columns[m] == rows[k], 1, 0), axis=0, keepdims=True)
        target = ids_ref[k : k + 1, :] * cap + rank
        pair = pair_ref[k : k + 1, :].astype(F32)
        match = jnp.broadcast_to(target, (tok, tok)).T[:, 0:1] == slot
        pairs = jnp.broadcast_to(pair, (tok, tok)).T[:, 0:1]
        source = source + jnp.sum(jnp.where(match, token - tok, 0), axis=0, keepdims=True)
        weight = weight + jnp.sum(jnp.where(match, pairs, 0.0), axis=0, keepdims=True)
        index_v[1 + k : 2 + k, 0:tok] = target
        weight_v[1 + k : 2 + k, 0:tok] = pair
    index_v[0:1, :] = source
    weight_v[0:1, :] = weight


def copy_kernel(*refs):
    n = (len(refs) - 1) // 2
    sems = refs[-1]
    copies = [pltpu.make_async_copy(refs[i], refs[n + i], sems.at[i]) for i in range(n)]
    for copy in copies:
        copy.start()
    for copy in copies:
        copy.wait()


def per_device(n_rep, n_ep, tokens, expert_ids, route_weights, w_gate_up, w_down, grad_out):
    tok, width = tokens.shape
    top = expert_ids.shape[1]
    hidden = w_down.shape[2]
    cap = 5 * tok * top // (4 * n_ep)
    slots = n_ep * cap
    quarter = width // n_rep
    half = quarter // 2
    tiles = width // LANES
    padded = -(-slots // LANES) * LANES
    vmem = pl.BlockSpec(memory_space=pltpu.VMEM)
    anywhere = pl.BlockSpec(memory_space=pl.ANY)
    V = pltpu.VMEM
    rows = V((slots, tiles, LANES), BF16)
    dma = pltpu.SemaphoreType.DMA
    shapes = (
        ((tok, width), BF16),
        ((tok, width), BF16),
        ((quarter, 2 * hidden), BF16),
        ((quarter, hidden), BF16),
        ((top, tok), F32),
    )
    made = pl.pallas_call(
        functools.partial(layer_kernel, (n_rep, n_ep, cap, tok, width, hidden)),
        out_shape=tuple(V(*shape) for shape in shapes),
        in_specs=[vmem] * 4 + [anywhere] * 2,
        out_specs=[vmem] * 5,
        scratch_shapes=[
            V((n_rep, quarter, 2 * hidden), BF16),
            V((n_rep, quarter, hidden), BF16),
            V((quarter, 2 * hidden), F32),
            V((quarter, hidden), F32),
            V((n_rep - 1, quarter, 2 * hidden), BF16),
            V((n_rep - 1, quarter, hidden), BF16),
            V((2, half, 2 * hidden), BF16),
            V((2, half, hidden), BF16),
            V((2, quarter, 2 * hidden), BF16),
            V((2, quarter, hidden), BF16),
        ]
        + [rows] * 8
        + [
            V((n_rep, slots, quarter), BF16),
            V((n_rep, slots, quarter), BF16),
            V((slots * tiles, LANES), F32),
            V((slots, 2 * hidden), F32),
            V((slots, hidden), F32),
            V((slots, hidden), BF16),
            V((slots, 2 * hidden), BF16),
            V((tok + 1, tiles, LANES), BF16),
            V((tok + 1, tiles, LANES), BF16),
            V((tok, LANES), F32),
            V((tok, LANES), F32),
            V((8, padded), jnp.int32),
            V((8, padded), F32),
            pltpu.SMEM((8, padded), jnp.int32),
            pltpu.SMEM((8, padded), F32),
            dma((4,)),
            dma((2, 2, 2)),
            dma((2, 2, 2)),
            dma((2, 2)),
            dma((2, 2)),
            dma((2, 2)),
            dma((2, 2)),
            dma((2, 2, 2)),
            dma((2, 2, 2)),
            dma((4,)),
            dma((4,)),
        ],
        compiler_params=pltpu.CompilerParams(
            collective_id=0, has_side_effects=True, vmem_limit_bytes=62000000
        ),
    )(expert_ids.T, route_weights.T, tokens, grad_out, w_gate_up[0], w_down[0])
    mixed, gtok, ggu, gdn, rg = pl.pallas_call(
        copy_kernel,
        out_shape=tuple(jax.ShapeDtypeStruct(*shape) for shape in shapes),
        in_specs=[vmem] * 5,
        out_specs=[anywhere] * 5,
        scratch_shapes=[dma((5,))],
        compiler_params=pltpu.CompilerParams(vmem_limit_bytes=1 << 20),
    )(*made)
    return mixed, gtok, ggu[None], gdn[None], rg.T


def solution(mesh):
    both = ("rep", "ep")
    split = P(both, None)
    weights = P("ep", "rep", None)
    return jax.shard_map(
        functools.partial(per_device, mesh.shape["rep"], mesh.shape["ep"]),
        mesh=mesh,
        in_specs=(split, split, split, weights, weights, split),
        out_specs=(split, split, weights, weights, split),
        check_vma=False,
    )
```

```python
import functools

import jax
import jax.numpy as jnp
from jax import lax
from jax.experimental import pallas as pl
from jax.experimental.pallas import tpu as pltpu
from jax.sharding import PartitionSpec as P

MESH = pl.DeviceIdType.MESH
F32 = jnp.float32
BF16 = jnp.bfloat16
LANES = 128


def layer_kernel(
    sizes,
    ids_ref,
    pair_ref,
    tokens_ref,
    grad_ref,
    wg_hbm,
    wd_hbm,
    mixed_ref,
    gtok_ref,
    ggu_ref,
    gdn_ref,
    rg_ref,
    wg,
    wd,
    part_g,
    part_d,
    pin_g,
    pin_d,
    home_g,
    home_d,
    relay_g,
    relay_d,
    back_g,
    back_d,
    din_g,
    din_d,
    send_x,
    recv_x,
    send_c,
    recv_c,
    send_o,
    recv_o,
    send_r,
    recv_r,
    x2,
    c2,
    scr,
    acc,
    gh,
    hid,
    ggu,
    tok_t,
    grd_t,
    rg_a,
    rg_b,
    index_v,
    weight_v,
    index_s,
    weight_s,
    local_sem,
    own_send,
    own_recv,
    out_send,
    out_recv,
    far_send,
    far_recv,
    fwd_send,
    fwd_recv,
    mate_send,
    mate_recv,
    swap_send,
    swap_recv,
    home_send,
    home_recv,
    near_send,
    near_recv,
    ret_send,
    ret_recv,
    fin_send,
    a2a_send,
    a2a_recv,
):
    n_rep, n_ep, cap, tok, width, hidden = sizes
    quarter = width // n_rep
    half = quarter // 2
    tiles = width // LANES
    per_q = quarter // LANES
    slots = n_ep * cap
    n_col = n_ep // 2
    x = lax.axis_index("rep")
    e = lax.axis_index("ep")
    col = e // 2
    core = lax.rem(e, 2)
    parity = lax.rem(x, 2)
    mate = 2 * col + 1 - core
    hosted = 2 * col + parity
    foreign = 2 * col + 1 - parity
    right = lax.rem(x + 1, n_rep)
    left = lax.rem(x + n_rep - 1, n_rep)
    ahead = lax.rem(x + 1 + 2 * core, n_rep)
    behind = lax.rem(x + 3 - 2 * core, n_rep)
    is_home = core == parity
    not_home = core != parity

    barrier = pltpu.get_barrier_semaphore()

    def greet(plane, index):
        pl.semaphore_signal(barrier, inc=1, device_id=(plane, index), device_id_type=MESH)

    greet(x, mate)
    greet(right, mate)
    greet(left, mate)
    greet(right, e)
    greet(left, e)

    @pl.loop(1, n_col)
    def _(i):
        other = 2 * lax.rem(col + i, n_col) + core
        greet(x, other)
        greet(right, other)
        greet(left, other)

    hbm = (wg_hbm, wd_hbm)
    full = (wg, wd)
    part = (part_g, part_d)
    pin = (pin_g, pin_d)
    home = (home_g, home_d)
    relay = (relay_g, relay_d)
    back = (back_g, back_d)
    din = (din_g, din_d)
    mine = pl.ds(pl.multiple_of(core * half, half), half)
    other_half = pl.ds(pl.multiple_of((1 - core) * half, half), half)
    halves = (pl.ds(0, half), pl.ds(half, half))
    sides = (right, left)

    def remote(src, dst, send, recv, plane, index):
        return pltpu.make_async_remote_copy(
            src_ref=src,
            dst_ref=dst,
            send_sem=send,
            recv_sem=recv,
            device_id=(plane, index),
            device_id_type=MESH,
        )

    def local_copy(k):
        return pltpu.make_async_copy(hbm[k], full[k].at[0], local_sem.at[k])

    def own_copy(k):
        return remote(hbm[k], full[k].at[0], own_send.at[k], own_recv.at[k], x, mate)

    def out_copy(k, d, h):
        return remote(
            hbm[k].at[halves[h], :],
            full[k].at[3 - 2 * d, halves[h], :],
            out_send.at[k, d, h],
            out_recv.at[k, d],
            sides[d],
            2 * col + h,
        )

    def far_copy(k, h):
        return remote(
            hbm[k].at[halves[h], :],
            relay[k],
            far_send.at[k, h],
            far_recv.at[k],
            sides[h],
            2 * col + h,
        )

    def fwd_copy(k):
        return remote(relay[k], full[k].at[2, mine, :], fwd_send.at[k], fwd_recv.at[k], ahead, e)

    def mate_copy(k, s):
        return remote(
            full[k].at[s, mine, :],
            full[k].at[s, mine, :],
            mate_send.at[k, s],
            mate_recv.at[k, s],
            x,
            mate,
        )

    def swap_copy(k, s):
        return remote(
            part[k].at[s, other_half, :],
            pin[k].at[s - 1],
            swap_send.at[k, s],
            swap_recv.at[k, s],
            x,
            mate,
        )

    def home_copy(k):
        return remote(part[k].at[0], home[k], home_send.at[k], home_recv.at[k], x, mate)

    def near_copy(k, d):
        return remote(
            part[k].at[1 + 2 * d, mine, :],
            din[k].at[d, mine, :],
            near_send.at[k, d],
            near_recv.at[k, d, core],
            sides[d],
            hosted,
        )

    def ret_copy(k):
        return remote(part[k].at[2, mine, :], back[k], ret_send.at[k], ret_recv.at[k], ahead, e)

    def fin_copy(k):
        return remote(
            back[k],
            din[k].at[0, mine, :],
            fin_send.at[k],
            near_recv.at[k, 0, core],
            ahead,
            foreign,
        )

    def send_rows(send, recv, n):
        def row_copy(plane, to, block, place):
            remote(
                send.at[pl.ds(block * cap, cap)],
                recv.at[pl.ds(place * cap, cap)],
                a2a_send.at[n],
                a2a_recv.at[n],
                plane,
                2 * to + core,
            ).start()

        row_copy(ahead, col, foreign, n_col + col)

        @pl.loop(1, n_col)
        def _(i):
            to = lax.rem(col + i, n_col)
            row_copy(x, to, 2 * to + parity, col)
            row_copy(ahead, to, 2 * to + 1 - parity, n_col + col)

        recv[pl.ds(col * cap, cap)] = send[pl.ds(hosted * cap, cap)]

    def return_rows(send, recv, n):
        def row_copy(plane, to, block):
            remote(
                send.at[pl.ds(block * cap, cap)],
                recv.at[pl.ds(hosted * cap, cap)],
                a2a_send.at[n],
                a2a_recv.at[n],
                plane,
                2 * to + core,
            ).start()

        row_copy(behind, col, n_col + col)

        @pl.loop(1, n_col)
        def _(i):
            to = lax.rem(col + i, n_col)
            row_copy(x, to, to)
            row_copy(behind, to, n_col + to)

        recv[pl.ds(hosted * cap, cap)] = send[pl.ds(col * cap, cap)]

    def wait_all(buf, sem):
        rest = buf.at[pl.ds(0, (n_ep - 1) * cap)]
        pltpu.make_async_copy(rest, rest, sem).wait()

    def tiled(src, dst):
        for j in range(tiles):
            scr[pl.ds(j, tok, stride=tiles), :] = src[:, j * LANES : (j + 1) * LANES].astype(F32)

        @pl.loop(0, tok // 8)
        def _(i):
            rows = pl.ds(pl.multiple_of(i * 8 * tiles, 16), 8 * tiles)
            dst[pl.ds(i * 8, 8)] = scr[rows, :].astype(BF16).reshape(8, tiles, LANES)

        dst[tok] = jnp.zeros((tiles, LANES), BF16)

    def row(r):
        return pl.ds(pl.multiple_of(r * tiles, 16), tiles)

    @pl.when(is_home)
    def _():
        for k in range(2):
            local_copy(k).start()

    tables = [
        pltpu.make_async_copy(index_v, index_s, local_sem.at[2]),
        pltpu.make_async_copy(weight_v, weight_s, local_sem.at[3]),
    ]
    routing(ids_ref, pair_ref, index_v, weight_v, cap)
    for copy in tables:
        copy.start()
    tiled(tokens_ref, tok_t)
    for copy in tables:
        copy.wait()

    @pl.loop(0, slots // 8)
    def _(i):
        for j in range(8):
            s = i * 8 + j
            send_x[s] = tok_t[index_s[0, s]]

    pl.semaphore_wait(barrier, 3 * n_col + 2)

    @pl.when(is_home)
    def _():
        for k in range(2):
            for h in range(2):
                far_copy(k, h).start()
        for k in range(2):
            own_copy(k).start()

    @pl.when(not_home)
    def _():
        for k in range(2):
            for h in range(2):
                for d in range(2):
                    out_copy(k, d, h).start()

    send_rows(send_x, recv_x, 0)
    tiled(grad_ref, grd_t)

    @pl.loop(0, slots // 8)
    def _(i):
        for j in range(8):
            s = i * 8 + j
            rows = grd_t[index_s[0, s]].astype(F32) * weight_s[0, s]
            send_c[s] = rows.astype(BF16)

    send_rows(send_c, recv_c, 1)

    def spread(recv, dst):
        @pl.loop(0, slots // 8)
        def _(i):
            rows = pl.ds(pl.multiple_of(i * 8 * tiles, 16), 8 * tiles)
            scr[rows, :] = recv[pl.ds(i * 8, 8)].astype(F32).reshape(8 * tiles, LANES)

        for q in range(n_rep):
            for j in range(per_q):
                dst[q, :, j * LANES : (j + 1) * LANES] = scr[
                    pl.ds(q * per_q + j, slots, stride=tiles), :
                ].astype(BF16)

    def place(s):
        return lax.rem(x + s, n_rep)

    def product(s, lhs, rhs, out, columns, step, first):
        @pl.loop(0, columns // step)
        def _(n):
            cols = pl.ds(pl.multiple_of(n * step, LANES), step)
            y = jnp.dot(lhs[place(s)], rhs[s, :, cols], preferred_element_type=F32)
            if first:
                out[:, cols] = y
            else:
                out[:, cols] = out[:, cols] + y

    def returned(lhs, rhs, send):
        for q in range(n_rep):
            s = lax.rem(q + n_rep - x, n_rep)
            for j in range(per_q):
                scr[pl.ds(q * per_q + j, slots, stride=tiles), :] = lax.dot_general(
                    lhs[...],
                    rhs[s, j * LANES : (j + 1) * LANES, :],
                    (((1,), (1,)), ((), ())),
                    preferred_element_type=F32,
                )

        @pl.loop(0, slots // 8)
        def _(i):
            rows = pl.ds(pl.multiple_of(i * 8 * tiles, 16), 8 * tiles)
            send[pl.ds(i * 8, 8)] = scr[rows, :].astype(BF16).reshape(8, tiles, LANES)

    def outer(lhs, rhs, s, rows, k, columns, step):
        block = lhs[place(s), :, rows]

        @pl.loop(0, columns // step)
        def _(n):
            cols = pl.ds(pl.multiple_of(n * step, LANES), step)
            y = lax.dot_general(
                block, rhs[:, cols], (((0,), (0,)), ((), ())), preferred_element_type=F32
            )
            part[k][s, rows, cols] = y.astype(BF16)

    def partial_grads(lhs, rhs, k, columns, step):
        for s in (2, 1, 3):
            outer(lhs, rhs, s, other_half, k, columns, step)
            swap_copy(k, s).start()
        for s in (2, 1, 3):
            outer(lhs, rhs, s, mine, k, columns, step)
            swap_copy(k, s).wait_recv()

            @pl.loop(0, half // 16)
            def _(i):
                here = pl.ds(pl.multiple_of(i * 16, 16), 16)
                there = pl.ds(pl.multiple_of(core * half + i * 16, 16), 16)
                total = part[k][s, there, :].astype(F32) + pin[k][s - 1, here, :].astype(F32)
                part[k][s, there, :] = total.astype(BF16)

            if s == 2:
                ret_copy(k).start()
            else:
                near_copy(k, s // 2).start()
        for h in range(2):
            outer(lhs, rhs, 0, halves[h], k, columns, step)

        @pl.when(not_home)
        def _():
            home_copy(k).start()

    def pass_on(k):
        ret_copy(k).wait_recv()
        fin_copy(k).start()

    def finish(k, out):
        @pl.when(is_home)
        def _():
            home_copy(k).wait_recv()

        for h in range(2):
            arrived = [
                remote(
                    back[k], din[k].at[d, halves[h], :], fin_send.at[k], near_recv.at[k, d, h], x, mate
                )
                for d in range(2)
            ]
            arrived[0].wait_recv()

            @pl.when(is_home)
            def _():
                @pl.loop(0, half // 16)
                def _(i):
                    rows = pl.ds(pl.multiple_of(h * half + i * 16, 16), 16)
                    total = part[k][0, rows, :].astype(F32) + home[k][rows, :].astype(F32)
                    out[rows, :] = (total + din[k][0, rows, :].astype(F32)).astype(BF16)

            @pl.when(not_home)
            def _():
                arrived[1].wait_recv()

                @pl.loop(0, half // 16)
                def _(i):
                    rows = pl.ds(pl.multiple_of(h * half + i * 16, 16), 16)
                    total = din[k][0, rows, :].astype(F32) + din[k][1, rows, :].astype(F32)
                    out[rows, :] = total.astype(BF16)

    def near_arrives(k):
        for d in range(2):
            out_copy(k, d, 0).wait_recv()
            mate_copy(k, 3 - 2 * d).start()

    def far_arrives(k):
        fwd_copy(k).wait_recv()
        mate_copy(k, 2).start()

    def own_arrives(k):
        @pl.when(is_home)
        def _():
            local_copy(k).wait()

        @pl.when(not_home)
        def _():
            own_copy(k).wait_recv()

    for k in range(2):
        far_copy(k, 0).wait_recv()
        fwd_copy(k).start()
    wait_all(recv_x, a2a_recv.at[0])
    spread(recv_x, x2)
    own_arrives(0)
    product(0, x2, wg, acc, 2 * hidden, 256, True)
    near_arrives(0)
    for s in (1, 3):
        mate_copy(0, s).wait_recv()
        product(s, x2, wg, acc, 2 * hidden, 256, False)
    near_arrives(1)
    far_arrives(0)
    mate_copy(0, 2).wait_recv()
    product(2, x2, wg, acc, 2 * hidden, 256, False)

    @pl.loop(0, slots // 16)
    def _(i):
        rows = pl.ds(pl.multiple_of(i * 16, 16), 16)
        gate = acc[rows, :hidden]
        up = acc[rows, hidden:]
        hid[rows, :] = (gate * jax.nn.sigmoid(gate) * up).astype(BF16)

    far_arrives(1)
    own_arrives(1)
    for s in (1, 3, 2):
        mate_copy(1, s).wait_recv()
    returned(hid, wd, send_o)
    return_rows(send_o, recv_o, 2)

    wait_all(recv_c, a2a_recv.at[1])
    spread(recv_c, c2)
    partial_grads(c2, hid, 1, hidden, 256)
    for s in range(n_rep):
        product(s, c2, wd, gh, hidden, 256, s == 0)

    @pl.loop(0, slots // 16)
    def _(i):
        rows = pl.ds(pl.multiple_of(i * 16, 16), 16)
        gate = acc[rows, :hidden]
        up = acc[rows, hidden:]
        grad = gh[rows, :]
        s = jax.nn.sigmoid(gate)
        ggu[rows, :hidden] = (grad * up * (s * (1.0 + gate * (1.0 - s)))).astype(BF16)
        ggu[rows, hidden:] = (grad * gate * s).astype(BF16)

    returned(ggu, wg, send_r)
    return_rows(send_r, recv_r, 3)
    pass_on(1)
    partial_grads(x2, ggu, 0, 2 * hidden, 256)

    def untiled(out):
        for j in range(tiles):
            out[:, j * LANES : (j + 1) * LANES] = scr[pl.ds(j, tok, stride=tiles), :].astype(BF16)

    wait_all(recv_o, a2a_recv.at[2])

    @pl.loop(0, tok // 4)
    def _(i):
        for j in range(4):
            t = i * 4 + j
            first = recv_o[index_s[1, t]].astype(F32)
            second = recv_o[index_s[2, t]].astype(F32)
            grad = grd_t[t].astype(F32)
            scr[row(t), :] = weight_s[1, t] * first + weight_s[2, t] * second
            rg_a[pl.ds(t, 1), :] = jnp.sum(grad * first, axis=0, keepdims=True)
            rg_b[pl.ds(t, 1), :] = jnp.sum(grad * second, axis=0, keepdims=True)

    untiled(mixed_ref)
    rg_ref[0:1, :] = jnp.sum(rg_a[...].T, axis=0, keepdims=True)
    rg_ref[1:2, :] = jnp.sum(rg_b[...].T, axis=0, keepdims=True)

    pass_on(0)
    finish(1, gdn_ref)
    wait_all(recv_r, a2a_recv.at[3])

    @pl.loop(0, tok // 4)
    def _(i):
        for j in range(4):
            t = i * 4 + j
            first = recv_r[index_s[1, t]].astype(F32)
            second = recv_r[index_s[2, t]].astype(F32)
            scr[row(t), :] = first + second

    untiled(gtok_ref)
    finish(0, ggu_ref)

    for n, buf in enumerate((send_x, send_c, send_o, send_r)):
        wait_all(buf, a2a_send.at[n])
    for k in range(2):
        fwd_copy(k).wait_send()
        ret_copy(k).wait_send()
        fin_copy(k).wait_send()
        for s in (1, 2, 3):
            mate_copy(k, s).wait_send()
            swap_copy(k, s).wait_send()
        for d in range(2):
            near_copy(k, d).wait_send()

    @pl.when(is_home)
    def _():
        for k in range(2):
            own_copy(k).wait_send()
            for h in range(2):
                far_copy(k, h).wait_send()

    @pl.when(not_home)
    def _():
        for k in range(2):
            home_copy(k).wait_send()
            for d in range(2):
                for h in range(2):
                    out_copy(k, d, h).wait_send()


def routing(ids_ref, pair_ref, index_v, weight_v, cap):
    top, tok = ids_ref.shape
    slots = index_v.shape[1]
    here = lax.broadcasted_iota(jnp.int32, (tok, tok), 0)
    there = lax.broadcasted_iota(jnp.int32, (tok, tok), 1)
    rows = [jnp.broadcast_to(ids_ref[k : k + 1, :], (tok, tok)) for k in range(top)]
    columns = [r.T for r in rows]
    slot = lax.broadcasted_iota(jnp.int32, (tok, slots), 1)
    token = lax.broadcasted_iota(jnp.int32, (tok, slots), 0)
    source = jnp.full((1, slots), tok, jnp.int32)
    weight = jnp.zeros((1, slots), F32)
    for k in range(top):
        rank = jnp.sum(
            jnp.where((columns[k] == rows[k]) & (here < there), 1, 0), axis=0, keepdims=True
        )
        for m in range(k):
            rank = rank + jnp.sum(jnp.where(columns[m] == rows[k], 1, 0), axis=0, keepdims=True)
        target = ids_ref[k : k + 1, :] * cap + rank
        pair = pair_ref[k : k + 1, :].astype(F32)
        match = jnp.broadcast_to(target, (tok, tok)).T[:, 0:1] == slot
        pairs = jnp.broadcast_to(pair, (tok, tok)).T[:, 0:1]
        source = source + jnp.sum(jnp.where(match, token - tok, 0), axis=0, keepdims=True)
        weight = weight + jnp.sum(jnp.where(match, pairs, 0.0), axis=0, keepdims=True)
        index_v[1 + k : 2 + k, 0:tok] = target
        weight_v[1 + k : 2 + k, 0:tok] = pair
    index_v[0:1, :] = source
    weight_v[0:1, :] = weight


def copy_kernel(*refs):
    n = (len(refs) - 1) // 2
    sems = refs[-1]
    copies = [pltpu.make_async_copy(refs[i], refs[n + i], sems.at[i]) for i in range(n)]
    for copy in copies:
        copy.start()
    for copy in copies:
        copy.wait()


def per_device(n_rep, n_ep, tokens, expert_ids, route_weights, w_gate_up, w_down, grad_out):
    tok, width = tokens.shape
    top = expert_ids.shape[1]
    hidden = w_down.shape[2]
    cap = 5 * tok * top // (4 * n_ep)
    slots = n_ep * cap
    quarter = width // n_rep
    half = quarter // 2
    tiles = width // LANES
    padded = -(-slots // LANES) * LANES
    vmem = pl.BlockSpec(memory_space=pltpu.VMEM)
    anywhere = pl.BlockSpec(memory_space=pl.ANY)
    V = pltpu.VMEM
    rows = V((slots, tiles, LANES), BF16)
    dma = pltpu.SemaphoreType.DMA
    shapes = (
        ((tok, width), BF16),
        ((tok, width), BF16),
        ((quarter, 2 * hidden), BF16),
        ((quarter, hidden), BF16),
        ((top, tok), F32),
    )
    made = pl.pallas_call(
        functools.partial(layer_kernel, (n_rep, n_ep, cap, tok, width, hidden)),
        out_shape=tuple(V(*shape) for shape in shapes),
        in_specs=[vmem] * 4 + [anywhere] * 2,
        out_specs=[vmem] * 5,
        scratch_shapes=[
            V(lead + (rows_, width_), BF16)
            for lead, rows_ in (
                ((n_rep,), quarter),
                ((n_rep,), quarter),
                ((n_rep - 1,), half),
                ((), quarter),
                ((), half),
                ((), half),
                ((2,), quarter),
            )
            for width_ in (2 * hidden, hidden)
        ]
        + [rows] * 8
        + [
            V((n_rep, slots, quarter), BF16),
            V((n_rep, slots, quarter), BF16),
            V((slots * tiles, LANES), F32),
            V((slots, 2 * hidden), F32),
            V((slots, hidden), F32),
            V((slots, hidden), BF16),
            V((slots, 2 * hidden), BF16),
            V((tok + 1, tiles, LANES), BF16),
            V((tok + 1, tiles, LANES), BF16),
            V((tok, LANES), F32),
            V((tok, LANES), F32),
            V((8, padded), jnp.int32),
            V((8, padded), F32),
            pltpu.SMEM((8, padded), jnp.int32),
            pltpu.SMEM((8, padded), F32),
            dma((4,)),
            dma((2,)),
            dma((2,)),
            dma((2, 2, 2)),
            dma((2, 2)),
            dma((2, 2)),
            dma((2,)),
            dma((2,)),
            dma((2,)),
            dma((2, n_rep)),
            dma((2, n_rep)),
            dma((2, n_rep)),
            dma((2, n_rep)),
            dma((2,)),
            dma((2,)),
            dma((2, 2)),
            dma((2, 2, 2)),
            dma((2,)),
            dma((2,)),
            dma((2,)),
            dma((4,)),
            dma((4,)),
        ],
        compiler_params=pltpu.CompilerParams(
            collective_id=0, has_side_effects=True, vmem_limit_bytes=62000000
        ),
    )(expert_ids.T, route_weights.T, tokens, grad_out, w_gate_up[0], w_down[0])
    mixed, gtok, ggu, gdn, rg = pl.pallas_call(
        copy_kernel,
        out_shape=tuple(jax.ShapeDtypeStruct(*shape) for shape in shapes),
        in_specs=[vmem] * 5,
        out_specs=[anywhere] * 5,
        scratch_shapes=[dma((5,))],
        compiler_params=pltpu.CompilerParams(vmem_limit_bytes=1 << 20),
    )(*made)
    return mixed, gtok, ggu[None], gdn[None], rg.T


def solution(mesh):
    both = ("rep", "ep")
    split = P(both, None)
    weights = P("ep", "rep", None)
    return jax.shard_map(
        functools.partial(per_device, mesh.shape["rep"], mesh.shape["ep"]),
        mesh=mesh,
        in_specs=(split, split, split, weights, weights, split),
        out_specs=(split, split, weights, weights, split),
        check_vma=False,
    )
```

```python
import functools

import jax
import jax.numpy as jnp
from jax import lax
from jax.experimental import pallas as pl
from jax.experimental.pallas import tpu as pltpu
from jax.sharding import PartitionSpec as P

MESH = pl.DeviceIdType.MESH
F32 = jnp.float32
BF16 = jnp.bfloat16
LANES = 128


def layer_kernel(
    sizes,
    ids_ref,
    pair_ref,
    tokens_ref,
    grad_ref,
    wg_hbm,
    wd_hbm,
    mixed_ref,
    gtok_ref,
    ggu_ref,
    gdn_ref,
    rg_ref,
    wg,
    wd,
    part_g,
    part_d,
    pin_g,
    pin_d,
    home_g,
    home_d,
    relay_g,
    relay_d,
    back_g,
    back_d,
    din_g,
    din_d,
    send_x,
    recv_x,
    send_c,
    recv_c,
    send_o,
    recv_o,
    send_r,
    recv_r,
    x2,
    c2,
    scr,
    acc,
    gh,
    hid,
    ggu,
    tok_t,
    grd_t,
    rg_a,
    rg_b,
    index_v,
    weight_v,
    index_s,
    weight_s,
    local_sem,
    own_send,
    own_recv,
    out_send,
    out_recv,
    far_send,
    far_recv,
    fwd_send,
    fwd_recv,
    mate_send,
    mate_recv,
    swap_send,
    swap_recv,
    home_send,
    home_recv,
    near_send,
    near_recv,
    ret_send,
    ret_recv,
    fin_send,
    a2a_send,
    a2a_recv,
    ready,
):
    n_rep, n_ep, cap, tok, width, hidden = sizes
    quarter = width // n_rep
    half = quarter // 2
    tiles = width // LANES
    per_q = quarter // LANES
    slots = n_ep * cap
    n_col = n_ep // 2
    x = lax.axis_index("rep")
    e = lax.axis_index("ep")
    col = e // 2
    core = lax.rem(e, 2)
    parity = lax.rem(x, 2)
    mate = 2 * col + 1 - core
    hosted = 2 * col + parity
    foreign = 2 * col + 1 - parity
    right = lax.rem(x + 1, n_rep)
    left = lax.rem(x + n_rep - 1, n_rep)
    ahead = lax.rem(x + 1 + 2 * core, n_rep)
    behind = lax.rem(x + 3 - 2 * core, n_rep)
    is_home = core == parity
    not_home = core != parity

    barrier = pltpu.get_barrier_semaphore()

    def greet(plane, index):
        pl.semaphore_signal(barrier, inc=1, device_id=(plane, index), device_id_type=MESH)

    ny, nz = 4, n_col // 4
    yy, zz = col // nz, lax.rem(col, nz)

    def beside(dy, dz):
        return (lax.rem(yy + dy, ny) * nz + lax.rem(zz + dz, nz)) * 2 + core

    near = [beside(1, 0), beside(ny - 1, 0), beside(0, 1), beside(0, nz - 1)]
    greet(x, mate)
    for plane in (right, left):
        greet(plane, mate)
        greet(plane, e)
    for index in near:
        greet(x, index)
    rounds = (
        [(x, index) for index in near],
        [(x, beside(0, 2)), (x, beside(0, nz - 2))],
        [(x, beside(dy, 0)) for dy in range(1, ny)],
        [(right, e), (left, e)],
    )

    def tell(r):
        for plane, index in rounds[r]:
            pl.semaphore_signal(
                ready.at[r], inc=1, device_id=(plane, index), device_id_type=MESH
            )

    def hear(r):
        pl.semaphore_wait(ready.at[r], len(rounds[r]))

    hbm = (wg_hbm, wd_hbm)
    full = (wg, wd)
    part = (part_g, part_d)
    pin = (pin_g, pin_d)
    home = (home_g, home_d)
    relay = (relay_g, relay_d)
    back = (back_g, back_d)
    din = (din_g, din_d)
    mine = pl.ds(pl.multiple_of(core * half, half), half)
    other_half = pl.ds(pl.multiple_of((1 - core) * half, half), half)
    halves = (pl.ds(0, half), pl.ds(half, half))
    sides = (right, left)

    def remote(src, dst, send, recv, plane, index):
        return pltpu.make_async_remote_copy(
            src_ref=src,
            dst_ref=dst,
            send_sem=send,
            recv_sem=recv,
            device_id=(plane, index),
            device_id_type=MESH,
        )

    def local_copy(k):
        return pltpu.make_async_copy(hbm[k], full[k].at[0], local_sem.at[k])

    def own_copy(k):
        return remote(hbm[k], full[k].at[0], own_send.at[k], own_recv.at[k], x, mate)

    def out_copy(k, d, h):
        return remote(
            hbm[k].at[halves[h], :],
            full[k].at[3 - 2 * d, halves[h], :],
            out_send.at[k, d, h],
            out_recv.at[k, d],
            sides[d],
            2 * col + h,
        )

    def far_copy(k, h):
        return remote(
            hbm[k].at[halves[h], :],
            relay[k],
            far_send.at[k, h],
            far_recv.at[k],
            sides[h],
            2 * col + h,
        )

    def fwd_copy(k):
        return remote(relay[k], full[k].at[2, mine, :], fwd_send.at[k], fwd_recv.at[k], ahead, e)

    def mate_copy(k, s):
        return remote(
            full[k].at[s, mine, :],
            full[k].at[s, mine, :],
            mate_send.at[k, s],
            mate_recv.at[k, s],
            x,
            mate,
        )

    def swap_copy(k, s):
        return remote(
            part[k].at[s, other_half, :],
            pin[k].at[s - 1],
            swap_send.at[k, s],
            swap_recv.at[k, s],
            x,
            mate,
        )

    def home_copy(k):
        return remote(part[k].at[0], home[k], home_send.at[k], home_recv.at[k], x, mate)

    def near_copy(k, d):
        return remote(
            part[k].at[1 + 2 * d, mine, :],
            din[k].at[d, mine, :],
            near_send.at[k, d],
            near_recv.at[k, d, core],
            sides[d],
            hosted,
        )

    def ret_copy(k):
        return remote(part[k].at[2, mine, :], back[k], ret_send.at[k], ret_recv.at[k], ahead, e)

    def fin_copy(k):
        return remote(
            back[k],
            din[k].at[0, mine, :],
            fin_send.at[k],
            near_recv.at[k, 0, core],
            ahead,
            foreign,
        )

    def send_rows(send, recv, n):
        def row_copy(plane, to, block, place):
            remote(
                send.at[pl.ds(block * cap, cap)],
                recv.at[pl.ds(place * cap, cap)],
                a2a_send.at[n],
                a2a_recv.at[n],
                plane,
                2 * to + core,
            ).start()

        row_copy(ahead, col, foreign, n_col + col)

        @pl.loop(1, n_col)
        def _(i):
            to = lax.rem(col + i, n_col)
            row_copy(x, to, 2 * to + parity, col)
            row_copy(ahead, to, 2 * to + 1 - parity, n_col + col)

        recv[pl.ds(col * cap, cap)] = send[pl.ds(hosted * cap, cap)]

    def return_rows(send, recv, n):
        def row_copy(plane, to, block):
            remote(
                send.at[pl.ds(block * cap, cap)],
                recv.at[pl.ds(hosted * cap, cap)],
                a2a_send.at[n],
                a2a_recv.at[n],
                plane,
                2 * to + core,
            ).start()

        row_copy(behind, col, n_col + col)

        @pl.loop(1, n_col)
        def _(i):
            to = lax.rem(col + i, n_col)
            row_copy(x, to, to)
            row_copy(behind, to, n_col + to)

        recv[pl.ds(hosted * cap, cap)] = send[pl.ds(col * cap, cap)]

    def wait_all(buf, sem):
        rest = buf.at[pl.ds(0, (n_ep - 1) * cap)]
        pltpu.make_async_copy(rest, rest, sem).wait()

    def tiled(src, dst):
        for j in range(tiles):
            scr[pl.ds(j, tok, stride=tiles), :] = src[:, j * LANES : (j + 1) * LANES].astype(F32)

        @pl.loop(0, tok // 8)
        def _(i):
            rows = pl.ds(pl.multiple_of(i * 8 * tiles, 16), 8 * tiles)
            dst[pl.ds(i * 8, 8)] = scr[rows, :].astype(BF16).reshape(8, tiles, LANES)

        dst[tok] = jnp.zeros((tiles, LANES), BF16)

    def row(r):
        return pl.ds(pl.multiple_of(r * tiles, 16), tiles)

    @pl.when(is_home)
    def _():
        for k in range(2):
            local_copy(k).start()

    pl.semaphore_wait(barrier, 9)

    @pl.when(is_home)
    def _():
        for k in range(2):
            for h in range(2):
                far_copy(k, h).start()
        for k in range(2):
            own_copy(k).start()

    @pl.when(not_home)
    def _():
        for k in range(2):
            for h in range(2):
                for d in range(2):
                    out_copy(k, d, h).start()

    tell(0)
    tables = [
        pltpu.make_async_copy(index_v, index_s, local_sem.at[2]),
        pltpu.make_async_copy(weight_v, weight_s, local_sem.at[3]),
    ]
    routing(ids_ref, pair_ref, index_v, weight_v, cap)
    for copy in tables:
        copy.start()
    hear(0)
    tell(1)
    tiled(tokens_ref, tok_t)
    hear(1)
    tell(2)
    for copy in tables:
        copy.wait()

    @pl.loop(0, slots // 8)
    def _(i):
        for j in range(8):
            s = i * 8 + j
            send_x[s] = tok_t[index_s[0, s]]

    hear(2)
    tell(3)
    tiled(grad_ref, grd_t)
    hear(3)
    send_rows(send_x, recv_x, 0)

    @pl.loop(0, slots // 8)
    def _(i):
        for j in range(8):
            s = i * 8 + j
            rows = grd_t[index_s[0, s]].astype(F32) * weight_s[0, s]
            send_c[s] = rows.astype(BF16)

    send_rows(send_c, recv_c, 1)

    def spread(recv, dst):
        @pl.loop(0, slots // 8)
        def _(i):
            rows = pl.ds(pl.multiple_of(i * 8 * tiles, 16), 8 * tiles)
            scr[rows, :] = recv[pl.ds(i * 8, 8)].astype(F32).reshape(8 * tiles, LANES)

        for q in range(n_rep):
            for j in range(per_q):
                dst[q, :, j * LANES : (j + 1) * LANES] = scr[
                    pl.ds(q * per_q + j, slots, stride=tiles), :
                ].astype(BF16)

    def place(s):
        return lax.rem(x + s, n_rep)

    def product(s, lhs, rhs, out, columns, step, first):
        @pl.loop(0, columns // step)
        def _(n):
            cols = pl.ds(pl.multiple_of(n * step, LANES), step)
            y = jnp.dot(lhs[place(s)], rhs[s, :, cols], preferred_element_type=F32)
            if first:
                out[:, cols] = y
            else:
                out[:, cols] = out[:, cols] + y

    def returned(lhs, rhs, send):
        for q in range(n_rep):
            s = lax.rem(q + n_rep - x, n_rep)
            for j in range(per_q):
                scr[pl.ds(q * per_q + j, slots, stride=tiles), :] = lax.dot_general(
                    lhs[...],
                    rhs[s, j * LANES : (j + 1) * LANES, :],
                    (((1,), (1,)), ((), ())),
                    preferred_element_type=F32,
                )

        @pl.loop(0, slots // 8)
        def _(i):
            rows = pl.ds(pl.multiple_of(i * 8 * tiles, 16), 8 * tiles)
            send[pl.ds(i * 8, 8)] = scr[rows, :].astype(BF16).reshape(8, tiles, LANES)

    def outer(lhs, rhs, s, rows, k, columns, step):
        block = lhs[place(s), :, rows]

        @pl.loop(0, columns // step)
        def _(n):
            cols = pl.ds(pl.multiple_of(n * step, LANES), step)
            y = lax.dot_general(
                block, rhs[:, cols], (((0,), (0,)), ((), ())), preferred_element_type=F32
            )
            part[k][s, rows, cols] = y.astype(BF16)

    def partial_grads(lhs, rhs, k, columns, step):
        for s in (2, 1, 3):
            outer(lhs, rhs, s, other_half, k, columns, step)
            swap_copy(k, s).start()
        for s in (2, 1, 3):
            outer(lhs, rhs, s, mine, k, columns, step)
            swap_copy(k, s).wait_recv()

            @pl.loop(0, half // 16)
            def _(i):
                here = pl.ds(pl.multiple_of(i * 16, 16), 16)
                there = pl.ds(pl.multiple_of(core * half + i * 16, 16), 16)
                total = part[k][s, there, :].astype(F32) + pin[k][s - 1, here, :].astype(F32)
                part[k][s, there, :] = total.astype(BF16)

            if s == 2:
                ret_copy(k).start()
            else:
                near_copy(k, s // 2).start()
        for h in range(2):
            outer(lhs, rhs, 0, halves[h], k, columns, step)

        @pl.when(not_home)
        def _():
            home_copy(k).start()

    def pass_on(k):
        ret_copy(k).wait_recv()
        fin_copy(k).start()

    def finish(k, out):
        @pl.when(is_home)
        def _():
            home_copy(k).wait_recv()

        for h in range(2):
            arrived = [
                remote(
                    back[k], din[k].at[d, halves[h], :], fin_send.at[k], near_recv.at[k, d, h], x, mate
                )
                for d in range(2)
            ]
            arrived[0].wait_recv()

            @pl.when(is_home)
            def _():
                @pl.loop(0, half // 16)
                def _(i):
                    rows = pl.ds(pl.multiple_of(h * half + i * 16, 16), 16)
                    total = part[k][0, rows, :].astype(F32) + home[k][rows, :].astype(F32)
                    out[rows, :] = (total + din[k][0, rows, :].astype(F32)).astype(BF16)

            @pl.when(not_home)
            def _():
                arrived[1].wait_recv()

                @pl.loop(0, half // 16)
                def _(i):
                    rows = pl.ds(pl.multiple_of(h * half + i * 16, 16), 16)
                    total = din[k][0, rows, :].astype(F32) + din[k][1, rows, :].astype(F32)
                    out[rows, :] = total.astype(BF16)

    def near_arrives(k):
        for d in range(2):
            out_copy(k, d, 0).wait_recv()
            mate_copy(k, 3 - 2 * d).start()

    def far_arrives(k):
        fwd_copy(k).wait_recv()
        mate_copy(k, 2).start()

    def own_arrives(k):
        @pl.when(is_home)
        def _():
            local_copy(k).wait()

        @pl.when(not_home)
        def _():
            own_copy(k).wait_recv()

    for k in range(2):
        far_copy(k, 0).wait_recv()
        fwd_copy(k).start()
    wait_all(recv_x, a2a_recv.at[0])
    spread(recv_x, x2)
    own_arrives(0)
    product(0, x2, wg, acc, 2 * hidden, 768, True)
    near_arrives(0)
    for s in (1, 3):
        mate_copy(0, s).wait_recv()
        product(s, x2, wg, acc, 2 * hidden, 768, False)
    near_arrives(1)
    far_arrives(0)
    mate_copy(0, 2).wait_recv()
    product(2, x2, wg, acc, 2 * hidden, 768, False)

    @pl.loop(0, slots // 16)
    def _(i):
        rows = pl.ds(pl.multiple_of(i * 16, 16), 16)
        gate = acc[rows, :hidden]
        up = acc[rows, hidden:]
        hid[rows, :] = (gate * jax.nn.sigmoid(gate) * up).astype(BF16)

    far_arrives(1)
    own_arrives(1)
    for s in (1, 3, 2):
        mate_copy(1, s).wait_recv()
    returned(hid, wd, send_o)
    return_rows(send_o, recv_o, 2)

    wait_all(recv_c, a2a_recv.at[1])
    spread(recv_c, c2)
    partial_grads(c2, hid, 1, hidden, 768)
    for s in range(n_rep):
        product(s, c2, wd, gh, hidden, 768, s == 0)

    @pl.loop(0, slots // 16)
    def _(i):
        rows = pl.ds(pl.multiple_of(i * 16, 16), 16)
        gate = acc[rows, :hidden]
        up = acc[rows, hidden:]
        grad = gh[rows, :]
        s = jax.nn.sigmoid(gate)
        ggu[rows, :hidden] = (grad * up * (s * (1.0 + gate * (1.0 - s)))).astype(BF16)
        ggu[rows, hidden:] = (grad * gate * s).astype(BF16)

    returned(ggu, wg, send_r)
    return_rows(send_r, recv_r, 3)
    pass_on(1)
    partial_grads(x2, ggu, 0, 2 * hidden, 768)

    def untiled(out):
        for j in range(tiles):
            out[:, j * LANES : (j + 1) * LANES] = scr[pl.ds(j, tok, stride=tiles), :].astype(BF16)

    wait_all(recv_o, a2a_recv.at[2])

    @pl.loop(0, tok // 4)
    def _(i):
        for j in range(4):
            t = i * 4 + j
            first = recv_o[index_s[1, t]].astype(F32)
            second = recv_o[index_s[2, t]].astype(F32)
            grad = grd_t[t].astype(F32)
            scr[row(t), :] = weight_s[1, t] * first + weight_s[2, t] * second
            rg_a[pl.ds(t, 1), :] = jnp.sum(grad * first, axis=0, keepdims=True)
            rg_b[pl.ds(t, 1), :] = jnp.sum(grad * second, axis=0, keepdims=True)

    untiled(mixed_ref)
    rg_ref[0:1, :] = jnp.sum(rg_a[...].T, axis=0, keepdims=True)
    rg_ref[1:2, :] = jnp.sum(rg_b[...].T, axis=0, keepdims=True)

    pass_on(0)
    finish(1, gdn_ref)
    wait_all(recv_r, a2a_recv.at[3])

    @pl.loop(0, tok // 4)
    def _(i):
        for j in range(4):
            t = i * 4 + j
            first = recv_r[index_s[1, t]].astype(F32)
            second = recv_r[index_s[2, t]].astype(F32)
            scr[row(t), :] = first + second

    untiled(gtok_ref)
    finish(0, ggu_ref)

    for n, buf in enumerate((send_x, send_c, send_o, send_r)):
        wait_all(buf, a2a_send.at[n])
    for k in range(2):
        fwd_copy(k).wait_send()
        ret_copy(k).wait_send()
        fin_copy(k).wait_send()
        for s in (1, 2, 3):
            mate_copy(k, s).wait_send()
            swap_copy(k, s).wait_send()
        for d in range(2):
            near_copy(k, d).wait_send()

    @pl.when(is_home)
    def _():
        for k in range(2):
            own_copy(k).wait_send()
            for h in range(2):
                far_copy(k, h).wait_send()

    @pl.when(not_home)
    def _():
        for k in range(2):
            home_copy(k).wait_send()
            for d in range(2):
                for h in range(2):
                    out_copy(k, d, h).wait_send()


def routing(ids_ref, pair_ref, index_v, weight_v, cap):
    top, tok = ids_ref.shape
    slots = index_v.shape[1]
    here = lax.broadcasted_iota(jnp.int32, (tok, tok), 0)
    there = lax.broadcasted_iota(jnp.int32, (tok, tok), 1)
    rows = [jnp.broadcast_to(ids_ref[k : k + 1, :], (tok, tok)) for k in range(top)]
    columns = [r.T for r in rows]
    slot = lax.broadcasted_iota(jnp.int32, (tok, slots), 1)
    token = lax.broadcasted_iota(jnp.int32, (tok, slots), 0)
    source = jnp.full((1, slots), tok, jnp.int32)
    weight = jnp.zeros((1, slots), F32)
    for k in range(top):
        rank = jnp.sum(
            jnp.where((columns[k] == rows[k]) & (here < there), 1, 0), axis=0, keepdims=True
        )
        for m in range(k):
            rank = rank + jnp.sum(jnp.where(columns[m] == rows[k], 1, 0), axis=0, keepdims=True)
        target = ids_ref[k : k + 1, :] * cap + rank
        pair = pair_ref[k : k + 1, :].astype(F32)
        match = jnp.broadcast_to(target, (tok, tok)).T[:, 0:1] == slot
        pairs = jnp.broadcast_to(pair, (tok, tok)).T[:, 0:1]
        source = source + jnp.sum(jnp.where(match, token - tok, 0), axis=0, keepdims=True)
        weight = weight + jnp.sum(jnp.where(match, pairs, 0.0), axis=0, keepdims=True)
        index_v[1 + k : 2 + k, 0:tok] = target
        weight_v[1 + k : 2 + k, 0:tok] = pair
    index_v[0:1, :] = source
    weight_v[0:1, :] = weight


def copy_kernel(*refs):
    n = (len(refs) - 1) // 2
    sems = refs[-1]
    copies = [pltpu.make_async_copy(refs[i], refs[n + i], sems.at[i]) for i in range(n)]
    for copy in copies:
        copy.start()
    for copy in copies:
        copy.wait()


def per_device(n_rep, n_ep, tokens, expert_ids, route_weights, w_gate_up, w_down, grad_out):
    tok, width = tokens.shape
    top = expert_ids.shape[1]
    hidden = w_down.shape[2]
    cap = 5 * tok * top // (4 * n_ep)
    slots = n_ep * cap
    quarter = width // n_rep
    half = quarter // 2
    tiles = width // LANES
    padded = -(-slots // LANES) * LANES
    vmem = pl.BlockSpec(memory_space=pltpu.VMEM)
    anywhere = pl.BlockSpec(memory_space=pl.ANY)
    V = pltpu.VMEM
    rows = V((slots, tiles, LANES), BF16)
    dma = pltpu.SemaphoreType.DMA
    shapes = (
        ((tok, width), BF16),
        ((tok, width), BF16),
        ((quarter, 2 * hidden), BF16),
        ((quarter, hidden), BF16),
        ((top, tok), F32),
    )
    made = pl.pallas_call(
        functools.partial(layer_kernel, (n_rep, n_ep, cap, tok, width, hidden)),
        out_shape=tuple(V(*shape) for shape in shapes),
        in_specs=[vmem] * 4 + [anywhere] * 2,
        out_specs=[vmem] * 5,
        scratch_shapes=[
            V(lead + (rows_, width_), BF16)
            for lead, rows_ in (
                ((n_rep,), quarter),
                ((n_rep,), quarter),
                ((n_rep - 1,), half),
                ((), quarter),
                ((), half),
                ((), half),
                ((2,), quarter),
            )
            for width_ in (2 * hidden, hidden)
        ]
        + [rows] * 8
        + [
            V((n_rep, slots, quarter), BF16),
            V((n_rep, slots, quarter), BF16),
            V((slots * tiles, LANES), F32),
            V((slots, 2 * hidden), F32),
            V((slots, hidden), F32),
            V((slots, hidden), BF16),
            V((slots, 2 * hidden), BF16),
            V((tok + 1, tiles, LANES), BF16),
            V((tok + 1, tiles, LANES), BF16),
            V((tok, LANES), F32),
            V((tok, LANES), F32),
            V((8, padded), jnp.int32),
            V((8, padded), F32),
            pltpu.SMEM((8, padded), jnp.int32),
            pltpu.SMEM((8, padded), F32),
            dma((4,)),
            dma((2,)),
            dma((2,)),
            dma((2, 2, 2)),
            dma((2, 2)),
            dma((2, 2)),
            dma((2,)),
            dma((2,)),
            dma((2,)),
            dma((2, n_rep)),
            dma((2, n_rep)),
            dma((2, n_rep)),
            dma((2, n_rep)),
            dma((2,)),
            dma((2,)),
            dma((2, 2)),
            dma((2, 2, 2)),
            dma((2,)),
            dma((2,)),
            dma((2,)),
            dma((4,)),
            dma((4,)),
            pltpu.SemaphoreType.REGULAR((4,)),
        ],
        compiler_params=pltpu.CompilerParams(
            collective_id=0, has_side_effects=True, vmem_limit_bytes=62000000
        ),
    )(expert_ids.T, route_weights.T, tokens, grad_out, w_gate_up[0], w_down[0])
    mixed, gtok, ggu, gdn, rg = pl.pallas_call(
        copy_kernel,
        out_shape=tuple(jax.ShapeDtypeStruct(*shape) for shape in shapes),
        in_specs=[vmem] * 5,
        out_specs=[anywhere] * 5,
        scratch_shapes=[dma((5,))],
        compiler_params=pltpu.CompilerParams(vmem_limit_bytes=1 << 20),
    )(*made)
    return mixed, gtok, ggu[None], gdn[None], rg.T


def solution(mesh):
    both = ("rep", "ep")
    split = P(both, None)
    weights = P("ep", "rep", None)
    return jax.shard_map(
        functools.partial(per_device, mesh.shape["rep"], mesh.shape["ep"]),
        mesh=mesh,
        in_specs=(split, split, split, weights, weights, split),
        out_specs=(split, split, weights, weights, split),
        check_vma=False,
    )
```

```python
import functools

import jax
import jax.numpy as jnp
from jax import lax
from jax.experimental import pallas as pl
from jax.experimental.pallas import tpu as pltpu
from jax.sharding import PartitionSpec as P

MESH = pl.DeviceIdType.MESH
F32 = jnp.float32
BF16 = jnp.bfloat16
LANES = 128


def layer_kernel(
    sizes,
    ids_ref,
    pair_ref,
    tokens_ref,
    grad_ref,
    wg_hbm,
    wd_hbm,
    mixed_ref,
    gtok_ref,
    ggu_ref,
    gdn_ref,
    rg_ref,
    wg,
    wd,
    part_g,
    part_d,
    pin_g,
    pin_d,
    home_g,
    home_d,
    relay_g,
    relay_d,
    back_g,
    back_d,
    din_g,
    din_d,
    send_x,
    recv_x,
    send_c,
    recv_c,
    send_o,
    recv_o,
    send_r,
    recv_r,
    x2,
    c2,
    scr,
    acc,
    gh,
    hid,
    ggu,
    tok_t,
    grd_t,
    rg_a,
    rg_b,
    index_v,
    weight_v,
    index_s,
    weight_s,
    local_sem,
    own_send,
    own_recv,
    out_send,
    out_recv,
    far_send,
    far_recv,
    fwd_send,
    fwd_recv,
    mate_send,
    mate_recv,
    swap_send,
    swap_recv,
    home_send,
    home_recv,
    near_send,
    near_recv,
    ret_send,
    ret_recv,
    fin_send,
    a2a_send,
    a2a_recv,
    ready,
):
    n_rep, n_ep, cap, tok, width, hidden = sizes
    quarter = width // n_rep
    half = quarter // 2
    tiles = width // LANES
    per_q = quarter // LANES
    slots = n_ep * cap
    n_col = n_ep // 2
    x = lax.axis_index("rep")
    e = lax.axis_index("ep")
    col = e // 2
    core = lax.rem(e, 2)
    parity = lax.rem(x, 2)
    mate = 2 * col + 1 - core
    hosted = 2 * col + parity
    foreign = 2 * col + 1 - parity
    right = lax.rem(x + 1, n_rep)
    left = lax.rem(x + n_rep - 1, n_rep)
    ahead = lax.rem(x + 1 + 2 * core, n_rep)
    behind = lax.rem(x + 3 - 2 * core, n_rep)
    is_home = core == parity
    not_home = core != parity

    barrier = pltpu.get_barrier_semaphore()

    def greet(plane, index):
        pl.semaphore_signal(barrier, inc=1, device_id=(plane, index), device_id_type=MESH)

    ny, nz = 4, n_col // 4
    yy, zz = col // nz, lax.rem(col, nz)

    def beside(dy, dz):
        return (lax.rem(yy + dy, ny) * nz + lax.rem(zz + dz, nz)) * 2 + core

    near = [beside(1, 0), beside(ny - 1, 0), beside(0, 1), beside(0, nz - 1)]
    greet(x, mate)
    for plane in (right, left):
        greet(plane, mate)
        greet(plane, e)
    for index in near:
        greet(x, index)
    rounds = (
        [(x, index) for index in near],
        [(x, beside(0, 2)), (x, beside(0, nz - 2))],
        [(x, beside(dy, 0)) for dy in range(1, ny)],
        [(right, e), (left, e)],
    )

    def tell(r):
        for plane, index in rounds[r]:
            pl.semaphore_signal(
                ready.at[r], inc=1, device_id=(plane, index), device_id_type=MESH
            )

    def hear(r):
        pl.semaphore_wait(ready.at[r], len(rounds[r]))

    hbm = (wg_hbm, wd_hbm)
    full = (wg, wd)
    part = (part_g, part_d)
    pin = (pin_g, pin_d)
    home = (home_g, home_d)
    relay = (relay_g, relay_d)
    back = (back_g, back_d)
    din = (din_g, din_d)
    mine = pl.ds(pl.multiple_of(core * half, half), half)
    other_half = pl.ds(pl.multiple_of((1 - core) * half, half), half)
    halves = (pl.ds(0, half), pl.ds(half, half))
    sides = (right, left)

    def remote(src, dst, send, recv, plane, index):
        return pltpu.make_async_remote_copy(
            src_ref=src,
            dst_ref=dst,
            send_sem=send,
            recv_sem=recv,
            device_id=(plane, index),
            device_id_type=MESH,
        )

    def local_copy(k):
        return pltpu.make_async_copy(hbm[k], full[k].at[0], local_sem.at[k])

    def own_copy(k):
        return remote(hbm[k], full[k].at[0], own_send.at[k], own_recv.at[k], x, mate)

    def out_copy(k, d, h):
        return remote(
            hbm[k].at[halves[h], :],
            full[k].at[3 - 2 * d, halves[h], :],
            out_send.at[k, d, h],
            out_recv.at[k, d],
            sides[d],
            2 * col + h,
        )

    def far_copy(k, h):
        return remote(
            hbm[k].at[halves[h], :],
            relay[k],
            far_send.at[k, h],
            far_recv.at[k],
            sides[h],
            2 * col + h,
        )

    def fwd_copy(k):
        return remote(relay[k], full[k].at[2, mine, :], fwd_send.at[k], fwd_recv.at[k], ahead, e)

    def mate_copy(k, s):
        return remote(
            full[k].at[s, mine, :],
            full[k].at[s, mine, :],
            mate_send.at[k, s],
            mate_recv.at[k, s],
            x,
            mate,
        )

    def swap_copy(k, s):
        return remote(
            part[k].at[s, other_half, :],
            pin[k].at[s - 1],
            swap_send.at[k, s],
            swap_recv.at[k, s],
            x,
            mate,
        )

    def home_copy(k):
        return remote(part[k].at[0], home[k], home_send.at[k], home_recv.at[k], x, mate)

    def near_copy(k, d):
        return remote(
            part[k].at[1 + 2 * d, mine, :],
            din[k].at[d, mine, :],
            near_send.at[k, d],
            near_recv.at[k, d, core],
            sides[d],
            hosted,
        )

    def ret_copy(k):
        return remote(part[k].at[2, mine, :], back[k], ret_send.at[k], ret_recv.at[k], ahead, e)

    def fin_copy(k):
        return remote(
            back[k],
            din[k].at[0, mine, :],
            fin_send.at[k],
            near_recv.at[k, 0, core],
            ahead,
            foreign,
        )

    def send_rows(send, recv, n):
        def row_copy(plane, to, block, place):
            remote(
                send.at[pl.ds(block * cap, cap)],
                recv.at[pl.ds(place * cap, cap)],
                a2a_send.at[n],
                a2a_recv.at[n],
                plane,
                2 * to + core,
            ).start()

        row_copy(ahead, col, foreign, n_col + col)

        @pl.loop(1, n_col)
        def _(i):
            to = lax.rem(col + i, n_col)
            row_copy(x, to, 2 * to + parity, col)
            row_copy(ahead, to, 2 * to + 1 - parity, n_col + col)

        recv[pl.ds(col * cap, cap)] = send[pl.ds(hosted * cap, cap)]

    def return_rows(send, recv, n):
        def row_copy(plane, to, block):
            remote(
                send.at[pl.ds(block * cap, cap)],
                recv.at[pl.ds(hosted * cap, cap)],
                a2a_send.at[n],
                a2a_recv.at[n],
                plane,
                2 * to + core,
            ).start()

        row_copy(behind, col, n_col + col)

        @pl.loop(1, n_col)
        def _(i):
            to = lax.rem(col + i, n_col)
            row_copy(x, to, to)
            row_copy(behind, to, n_col + to)

        recv[pl.ds(hosted * cap, cap)] = send[pl.ds(col * cap, cap)]

    def wait_all(buf, sem):
        rest = buf.at[pl.ds(0, (n_ep - 1) * cap)]
        pltpu.make_async_copy(rest, rest, sem).wait()

    def tiled(src, dst):
        for j in range(tiles):
            scr[pl.ds(j, tok, stride=tiles), :] = src[:, j * LANES : (j + 1) * LANES].astype(F32)

        @pl.loop(0, tok // 8)
        def _(i):
            rows = pl.ds(pl.multiple_of(i * 8 * tiles, 16), 8 * tiles)
            dst[pl.ds(i * 8, 8)] = scr[rows, :].astype(BF16).reshape(8, tiles, LANES)

        dst[tok] = jnp.zeros((tiles, LANES), BF16)

    def row(r):
        return pl.ds(pl.multiple_of(r * tiles, 16), tiles)

    @pl.when(is_home)
    def _():
        for k in range(2):
            local_copy(k).start()

    pl.semaphore_wait(barrier, 9)

    @pl.when(is_home)
    def _():
        for k in range(2):
            for h in range(2):
                far_copy(k, h).start()
        for k in range(2):
            own_copy(k).start()

    @pl.when(not_home)
    def _():
        for k in range(2):
            for h in range(2):
                for d in range(2):
                    out_copy(k, d, h).start()

    tell(0)
    tables = [
        pltpu.make_async_copy(index_v, index_s, local_sem.at[2]),
        pltpu.make_async_copy(weight_v, weight_s, local_sem.at[3]),
    ]
    routing(ids_ref, pair_ref, index_v, weight_v, cap)
    for copy in tables:
        copy.start()
    hear(0)
    tell(1)
    tiled(tokens_ref, tok_t)
    hear(1)
    tell(2)
    for copy in tables:
        copy.wait()

    @pl.loop(0, slots // 8)
    def _(i):
        for j in range(8):
            s = i * 8 + j
            send_x[s] = tok_t[index_s[0, s]]

    hear(2)
    tell(3)
    tiled(grad_ref, grd_t)
    hear(3)
    send_rows(send_x, recv_x, 0)

    @pl.loop(0, slots // 8)
    def _(i):
        for j in range(8):
            s = i * 8 + j
            rows = grd_t[index_s[0, s]].astype(F32) * weight_s[0, s]
            send_c[s] = rows.astype(BF16)

    send_rows(send_c, recv_c, 1)

    def spread(recv, dst):
        @pl.loop(0, slots // 8)
        def _(i):
            rows = pl.ds(pl.multiple_of(i * 8 * tiles, 16), 8 * tiles)
            scr[rows, :] = recv[pl.ds(i * 8, 8)].astype(F32).reshape(8 * tiles, LANES)

        for q in range(n_rep):
            for j in range(per_q):
                dst[q, :, j * LANES : (j + 1) * LANES] = scr[
                    pl.ds(q * per_q + j, slots, stride=tiles), :
                ].astype(BF16)

    def place(s):
        return lax.rem(x + s, n_rep)

    def product(s, lhs, rhs, out, columns, step, first):
        @pl.loop(0, columns // step)
        def _(n):
            cols = pl.ds(pl.multiple_of(n * step, LANES), step)
            y = jnp.dot(lhs[place(s)], rhs[s, :, cols], preferred_element_type=F32)
            if first:
                out[:, cols] = y
            else:
                out[:, cols] = out[:, cols] + y

    def returned(lhs, rhs, send):
        for q in range(n_rep):
            s = lax.rem(q + n_rep - x, n_rep)
            for j in range(per_q):
                scr[pl.ds(q * per_q + j, slots, stride=tiles), :] = lax.dot_general(
                    lhs[...],
                    rhs[s, j * LANES : (j + 1) * LANES, :],
                    (((1,), (1,)), ((), ())),
                    preferred_element_type=F32,
                )

        @pl.loop(0, slots // 8)
        def _(i):
            rows = pl.ds(pl.multiple_of(i * 8 * tiles, 16), 8 * tiles)
            send[pl.ds(i * 8, 8)] = scr[rows, :].astype(BF16).reshape(8, tiles, LANES)

    def outer(lhs, rhs, s, rows, k, columns, step):
        block = lhs[place(s), :, rows]

        @pl.loop(0, columns // step)
        def _(n):
            cols = pl.ds(pl.multiple_of(n * step, LANES), step)
            y = lax.dot_general(
                block, rhs[:, cols], (((0,), (0,)), ((), ())), preferred_element_type=F32
            )
            part[k][s, rows, cols] = y.astype(BF16)

    def partial_grads(lhs, rhs, k, columns, step):
        for s in (2, 1, 3):
            outer(lhs, rhs, s, other_half, k, columns, step)
            swap_copy(k, s).start()
        if k == 1:
            far_arrives(1)
        for s in (2, 1, 3):
            outer(lhs, rhs, s, mine, k, columns, step)
            swap_copy(k, s).wait_recv()

            @pl.loop(0, half // 16)
            def _(i):
                here = pl.ds(pl.multiple_of(i * 16, 16), 16)
                there = pl.ds(pl.multiple_of(core * half + i * 16, 16), 16)
                total = part[k][s, there, :].astype(F32) + pin[k][s - 1, here, :].astype(F32)
                part[k][s, there, :] = total.astype(BF16)

            if s == 2:
                ret_copy(k).start()
            else:
                near_copy(k, s // 2).start()

    def home_grads(lhs, rhs, k, columns, step):
        for h in range(2):
            outer(lhs, rhs, 0, halves[h], k, columns, step)

        @pl.when(not_home)
        def _():
            home_copy(k).start()

    def pass_on(k):
        ret_copy(k).wait_recv()
        fin_copy(k).start()

    def finish(k, out):
        @pl.when(is_home)
        def _():
            home_copy(k).wait_recv()

        for h in range(2):
            arrived = [
                remote(
                    back[k], din[k].at[d, halves[h], :], fin_send.at[k], near_recv.at[k, d, h], x, mate
                )
                for d in range(2)
            ]
            arrived[0].wait_recv()

            @pl.when(is_home)
            def _():
                @pl.loop(0, half // 16)
                def _(i):
                    rows = pl.ds(pl.multiple_of(h * half + i * 16, 16), 16)
                    total = part[k][0, rows, :].astype(F32) + home[k][rows, :].astype(F32)
                    out[rows, :] = (total + din[k][0, rows, :].astype(F32)).astype(BF16)

            @pl.when(not_home)
            def _():
                arrived[1].wait_recv()

                @pl.loop(0, half // 16)
                def _(i):
                    rows = pl.ds(pl.multiple_of(h * half + i * 16, 16), 16)
                    total = din[k][0, rows, :].astype(F32) + din[k][1, rows, :].astype(F32)
                    out[rows, :] = total.astype(BF16)

    def near_arrives(k):
        for d in range(2):
            out_copy(k, d, 0).wait_recv()
            mate_copy(k, 3 - 2 * d).start()

    def far_arrives(k):
        fwd_copy(k).wait_recv()
        mate_copy(k, 2).start()

    def own_arrives(k):
        @pl.when(is_home)
        def _():
            local_copy(k).wait()

        @pl.when(not_home)
        def _():
            own_copy(k).wait_recv()

    for k in range(2):
        far_copy(k, 0).wait_recv()
        fwd_copy(k).start()
    wait_all(recv_x, a2a_recv.at[0])
    spread(recv_x, x2)
    own_arrives(0)
    product(0, x2, wg, acc, 2 * hidden, 768, True)
    near_arrives(0)
    for s in (1, 3):
        mate_copy(0, s).wait_recv()
        product(s, x2, wg, acc, 2 * hidden, 768, False)
    near_arrives(1)
    far_arrives(0)
    mate_copy(0, 2).wait_recv()
    product(2, x2, wg, acc, 2 * hidden, 768, False)

    @pl.loop(0, slots // 16)
    def _(i):
        rows = pl.ds(pl.multiple_of(i * 16, 16), 16)
        gate = acc[rows, :hidden]
        up = acc[rows, hidden:]
        hid[rows, :] = (gate * jax.nn.sigmoid(gate) * up).astype(BF16)

    wait_all(recv_c, a2a_recv.at[1])
    spread(recv_c, c2)
    partial_grads(c2, hid, 1, hidden, 768)
    own_arrives(1)
    for s in (1, 3, 2):
        mate_copy(1, s).wait_recv()
    returned(hid, wd, send_o)
    return_rows(send_o, recv_o, 2)
    for s in range(n_rep):
        product(s, c2, wd, gh, hidden, 768, s == 0)

    @pl.loop(0, slots // 16)
    def _(i):
        rows = pl.ds(pl.multiple_of(i * 16, 16), 16)
        gate = acc[rows, :hidden]
        up = acc[rows, hidden:]
        grad = gh[rows, :]
        s = jax.nn.sigmoid(gate)
        ggu[rows, :hidden] = (grad * up * (s * (1.0 + gate * (1.0 - s)))).astype(BF16)
        ggu[rows, hidden:] = (grad * gate * s).astype(BF16)

    returned(ggu, wg, send_r)
    return_rows(send_r, recv_r, 3)
    pass_on(1)
    partial_grads(x2, ggu, 0, 2 * hidden, 768)
    home_grads(c2, hid, 1, hidden, 768)
    home_grads(x2, ggu, 0, 2 * hidden, 768)

    def untiled(out):
        for j in range(tiles):
            out[:, j * LANES : (j + 1) * LANES] = scr[pl.ds(j, tok, stride=tiles), :].astype(BF16)

    wait_all(recv_o, a2a_recv.at[2])

    @pl.loop(0, tok // 4)
    def _(i):
        for j in range(4):
            t = i * 4 + j
            first = recv_o[index_s[1, t]].astype(F32)
            second = recv_o[index_s[2, t]].astype(F32)
            grad = grd_t[t].astype(F32)
            scr[row(t), :] = weight_s[1, t] * first + weight_s[2, t] * second
            rg_a[pl.ds(t, 1), :] = jnp.sum(grad * first, axis=0, keepdims=True)
            rg_b[pl.ds(t, 1), :] = jnp.sum(grad * second, axis=0, keepdims=True)

    untiled(mixed_ref)
    rg_ref[0:1, :] = jnp.sum(rg_a[...].T, axis=0, keepdims=True)
    rg_ref[1:2, :] = jnp.sum(rg_b[...].T, axis=0, keepdims=True)

    pass_on(0)
    finish(1, gdn_ref)
    wait_all(recv_r, a2a_recv.at[3])

    @pl.loop(0, tok // 4)
    def _(i):
        for j in range(4):
            t = i * 4 + j
            first = recv_r[index_s[1, t]].astype(F32)
            second = recv_r[index_s[2, t]].astype(F32)
            scr[row(t), :] = first + second

    untiled(gtok_ref)
    finish(0, ggu_ref)

    for n, buf in enumerate((send_x, send_c, send_o, send_r)):
        wait_all(buf, a2a_send.at[n])
    for k in range(2):
        fwd_copy(k).wait_send()
        ret_copy(k).wait_send()
        fin_copy(k).wait_send()
        for s in (1, 2, 3):
            mate_copy(k, s).wait_send()
            swap_copy(k, s).wait_send()
        for d in range(2):
            near_copy(k, d).wait_send()

    @pl.when(is_home)
    def _():
        for k in range(2):
            own_copy(k).wait_send()
            for h in range(2):
                far_copy(k, h).wait_send()

    @pl.when(not_home)
    def _():
        for k in range(2):
            home_copy(k).wait_send()
            for d in range(2):
                for h in range(2):
                    out_copy(k, d, h).wait_send()


def routing(ids_ref, pair_ref, index_v, weight_v, cap):
    top, tok = ids_ref.shape
    slots = index_v.shape[1]
    here = lax.broadcasted_iota(jnp.int32, (tok, tok), 0)
    there = lax.broadcasted_iota(jnp.int32, (tok, tok), 1)
    rows = [jnp.broadcast_to(ids_ref[k : k + 1, :], (tok, tok)) for k in range(top)]
    columns = [r.T for r in rows]
    slot = lax.broadcasted_iota(jnp.int32, (tok, slots), 1)
    token = lax.broadcasted_iota(jnp.int32, (tok, slots), 0)
    source = jnp.full((1, slots), tok, jnp.int32)
    weight = jnp.zeros((1, slots), F32)
    for k in range(top):
        rank = jnp.sum(
            jnp.where((columns[k] == rows[k]) & (here < there), 1, 0), axis=0, keepdims=True
        )
        for m in range(k):
            rank = rank + jnp.sum(jnp.where(columns[m] == rows[k], 1, 0), axis=0, keepdims=True)
        target = ids_ref[k : k + 1, :] * cap + rank
        pair = pair_ref[k : k + 1, :].astype(F32)
        match = jnp.broadcast_to(target, (tok, tok)).T[:, 0:1] == slot
        pairs = jnp.broadcast_to(pair, (tok, tok)).T[:, 0:1]
        source = source + jnp.sum(jnp.where(match, token - tok, 0), axis=0, keepdims=True)
        weight = weight + jnp.sum(jnp.where(match, pairs, 0.0), axis=0, keepdims=True)
        index_v[1 + k : 2 + k, 0:tok] = target
        weight_v[1 + k : 2 + k, 0:tok] = pair
    index_v[0:1, :] = source
    weight_v[0:1, :] = weight


def copy_kernel(*refs):
    n = (len(refs) - 1) // 2
    sems = refs[-1]
    copies = [pltpu.make_async_copy(refs[i], refs[n + i], sems.at[i]) for i in range(n)]
    for copy in copies:
        copy.start()
    for copy in copies:
        copy.wait()


def per_device(n_rep, n_ep, tokens, expert_ids, route_weights, w_gate_up, w_down, grad_out):
    tok, width = tokens.shape
    top = expert_ids.shape[1]
    hidden = w_down.shape[2]
    cap = 5 * tok * top // (4 * n_ep)
    slots = n_ep * cap
    quarter = width // n_rep
    half = quarter // 2
    tiles = width // LANES
    padded = -(-slots // LANES) * LANES
    vmem = pl.BlockSpec(memory_space=pltpu.VMEM)
    anywhere = pl.BlockSpec(memory_space=pl.ANY)
    V = pltpu.VMEM
    rows = V((slots, tiles, LANES), BF16)
    dma = pltpu.SemaphoreType.DMA
    shapes = (
        ((tok, width), BF16),
        ((tok, width), BF16),
        ((quarter, 2 * hidden), BF16),
        ((quarter, hidden), BF16),
        ((top, tok), F32),
    )
    made = pl.pallas_call(
        functools.partial(layer_kernel, (n_rep, n_ep, cap, tok, width, hidden)),
        out_shape=tuple(V(*shape) for shape in shapes),
        in_specs=[vmem] * 4 + [anywhere] * 2,
        out_specs=[vmem] * 5,
        scratch_shapes=[
            V(lead + (rows_, width_), BF16)
            for lead, rows_ in (
                ((n_rep,), quarter),
                ((n_rep,), quarter),
                ((n_rep - 1,), half),
                ((), quarter),
                ((), half),
                ((), half),
                ((2,), quarter),
            )
            for width_ in (2 * hidden, hidden)
        ]
        + [rows] * 8
        + [
            V((n_rep, slots, quarter), BF16),
            V((n_rep, slots, quarter), BF16),
            V((slots * tiles, LANES), F32),
            V((slots, 2 * hidden), F32),
            V((slots, hidden), F32),
            V((slots, hidden), BF16),
            V((slots, 2 * hidden), BF16),
            V((tok + 1, tiles, LANES), BF16),
            V((tok + 1, tiles, LANES), BF16),
            V((tok, LANES), F32),
            V((tok, LANES), F32),
            V((8, padded), jnp.int32),
            V((8, padded), F32),
            pltpu.SMEM((8, padded), jnp.int32),
            pltpu.SMEM((8, padded), F32),
            dma((4,)),
            dma((2,)),
            dma((2,)),
            dma((2, 2, 2)),
            dma((2, 2)),
            dma((2, 2)),
            dma((2,)),
            dma((2,)),
            dma((2,)),
            dma((2, n_rep)),
            dma((2, n_rep)),
            dma((2, n_rep)),
            dma((2, n_rep)),
            dma((2,)),
            dma((2,)),
            dma((2, 2)),
            dma((2, 2, 2)),
            dma((2,)),
            dma((2,)),
            dma((2,)),
            dma((4,)),
            dma((4,)),
            pltpu.SemaphoreType.REGULAR((4,)),
        ],
        compiler_params=pltpu.CompilerParams(
            collective_id=0, has_side_effects=True, vmem_limit_bytes=62000000
        ),
    )(expert_ids.T, route_weights.T, tokens, grad_out, w_gate_up[0], w_down[0])
    mixed, gtok, ggu, gdn, rg = pl.pallas_call(
        copy_kernel,
        out_shape=tuple(jax.ShapeDtypeStruct(*shape) for shape in shapes),
        in_specs=[vmem] * 5,
        out_specs=[anywhere] * 5,
        scratch_shapes=[dma((5,))],
        compiler_params=pltpu.CompilerParams(vmem_limit_bytes=1 << 20),
    )(*made)
    return mixed, gtok, ggu[None], gdn[None], rg.T


def solution(mesh):
    both = ("rep", "ep")
    split = P(both, None)
    weights = P("ep", "rep", None)
    return jax.shard_map(
        functools.partial(per_device, mesh.shape["rep"], mesh.shape["ep"]),
        mesh=mesh,
        in_specs=(split, split, split, weights, weights, split),
        out_specs=(split, split, weights, weights, split),
        check_vma=False,
    )
```

```python
import functools

import jax
import jax.numpy as jnp
from jax import lax
from jax.experimental import pallas as pl
from jax.experimental.pallas import tpu as pltpu
from jax.sharding import PartitionSpec as P

MESH = pl.DeviceIdType.MESH
F32 = jnp.float32
BF16 = jnp.bfloat16
LANES = 128


def layer_kernel(
    sizes,
    ids_ref,
    pair_ref,
    tokens_ref,
    grad_ref,
    wg_hbm,
    wd_hbm,
    mixed_ref,
    gtok_ref,
    ggu_ref,
    gdn_ref,
    rg_ref,
    wg,
    wd,
    part_g,
    part_d,
    pin_g,
    pin_d,
    home_g,
    home_d,
    relay_g,
    relay_d,
    back_g,
    back_d,
    din_g,
    din_d,
    send_x,
    recv_x,
    send_c,
    recv_c,
    send_o,
    recv_o,
    send_r,
    recv_r,
    x2,
    c2,
    scr,
    acc,
    gh,
    hid,
    ggu,
    tok_t,
    grd_t,
    rg_a,
    rg_b,
    index_v,
    weight_v,
    index_s,
    weight_s,
    local_sem,
    own_send,
    own_recv,
    out_send,
    out_recv,
    far_send,
    far_recv,
    fwd_send,
    fwd_recv,
    mate_send,
    mate_recv,
    swap_send,
    swap_recv,
    home_send,
    home_recv,
    near_send,
    near_recv,
    ret_send,
    ret_recv,
    fin_send,
    a2a_send,
    a2a_recv,
    ready,
):
    n_rep, n_ep, cap, tok, width, hidden = sizes
    quarter = width // n_rep
    half = quarter // 2
    tiles = width // LANES
    per_q = quarter // LANES
    slots = n_ep * cap
    n_col = n_ep // 2
    x = lax.axis_index("rep")
    e = lax.axis_index("ep")
    col = e // 2
    core = lax.rem(e, 2)
    parity = lax.rem(x, 2)
    mate = 2 * col + 1 - core
    hosted = 2 * col + parity
    foreign = 2 * col + 1 - parity
    right = lax.rem(x + 1, n_rep)
    left = lax.rem(x + n_rep - 1, n_rep)
    ahead = lax.rem(x + 1 + 2 * core, n_rep)
    behind = lax.rem(x + 3 - 2 * core, n_rep)
    is_home = core == parity
    not_home = core != parity

    barrier = pltpu.get_barrier_semaphore()

    def greet(plane, index):
        pl.semaphore_signal(barrier, inc=1, device_id=(plane, index), device_id_type=MESH)

    ny, nz = 4, n_col // 4
    yy, zz = col // nz, lax.rem(col, nz)

    def beside(dy, dz):
        return (lax.rem(yy + dy, ny) * nz + lax.rem(zz + dz, nz)) * 2 + core

    near = [beside(1, 0), beside(ny - 1, 0), beside(0, 1), beside(0, nz - 1)]
    greet(x, mate)
    for plane in (right, left):
        greet(plane, mate)
        greet(plane, e)
    for index in near:
        greet(x, index)
    rounds = (
        [(x, index) for index in near],
        [(x, beside(0, 2)), (x, beside(0, nz - 2))],
        [(x, beside(dy, 0)) for dy in range(1, ny)],
        [(right, e), (left, e)],
    )

    def tell(r):
        for plane, index in rounds[r]:
            pl.semaphore_signal(
                ready.at[r], inc=1, device_id=(plane, index), device_id_type=MESH
            )

    def hear(r):
        pl.semaphore_wait(ready.at[r], len(rounds[r]))

    hbm = (wg_hbm, wd_hbm)
    full = (wg, wd)
    part = (part_g, part_d)
    pin = (pin_g, pin_d)
    home = (home_g, home_d)
    relay = (relay_g, relay_d)
    back = (back_g, back_d)
    din = (din_g, din_d)
    mine = pl.ds(pl.multiple_of(core * half, half), half)
    other_half = pl.ds(pl.multiple_of((1 - core) * half, half), half)
    halves = (pl.ds(0, half), pl.ds(half, half))
    sides = (right, left)

    def remote(src, dst, send, recv, plane, index):
        return pltpu.make_async_remote_copy(
            src_ref=src,
            dst_ref=dst,
            send_sem=send,
            recv_sem=recv,
            device_id=(plane, index),
            device_id_type=MESH,
        )

    def local_copy(k):
        return pltpu.make_async_copy(hbm[k], full[k].at[0], local_sem.at[k])

    def own_copy(k):
        return remote(hbm[k], full[k].at[0], own_send.at[k], own_recv.at[k], x, mate)

    def out_copy(k, d, h):
        return remote(
            hbm[k].at[halves[h], :],
            full[k].at[3 - 2 * d, halves[h], :],
            out_send.at[k, d, h],
            out_recv.at[k, d],
            sides[d],
            2 * col + h,
        )

    def far_copy(k, h):
        return remote(
            hbm[k].at[halves[h], :],
            relay[k],
            far_send.at[k, h],
            far_recv.at[k],
            sides[h],
            2 * col + h,
        )

    def fwd_copy(k):
        return remote(relay[k], full[k].at[2, mine, :], fwd_send.at[k], fwd_recv.at[k], ahead, e)

    def mate_copy(k, s):
        return remote(
            full[k].at[s, mine, :],
            full[k].at[s, mine, :],
            mate_send.at[k, s],
            mate_recv.at[k, s],
            x,
            mate,
        )

    def swap_copy(k, s):
        return remote(
            part[k].at[s, other_half, :],
            pin[k].at[s - 1],
            swap_send.at[k, s],
            swap_recv.at[k, s],
            x,
            mate,
        )

    def home_copy(k):
        return remote(part[k].at[0], home[k], home_send.at[k], home_recv.at[k], x, mate)

    def near_copy(k, d):
        return remote(
            part[k].at[1 + 2 * d, mine, :],
            din[k].at[d, mine, :],
            near_send.at[k, d],
            near_recv.at[k, d, core],
            sides[d],
            hosted,
        )

    def ret_copy(k):
        return remote(part[k].at[2, mine, :], back[k], ret_send.at[k], ret_recv.at[k], ahead, e)

    def fin_copy(k):
        return remote(
            back[k],
            din[k].at[0, mine, :],
            fin_send.at[k],
            near_recv.at[k, 0, core],
            ahead,
            foreign,
        )

    def send_rows(send, recv, n):
        def row_copy(plane, to, block, place):
            remote(
                send.at[pl.ds(block * cap, cap)],
                recv.at[pl.ds(place * cap, cap)],
                a2a_send.at[n],
                a2a_recv.at[n],
                plane,
                2 * to + core,
            ).start()

        row_copy(ahead, col, foreign, n_col + col)

        @pl.loop(1, n_col)
        def _(i):
            to = lax.rem(col + i, n_col)
            row_copy(x, to, 2 * to + parity, col)
            row_copy(ahead, to, 2 * to + 1 - parity, n_col + col)

        recv[pl.ds(col * cap, cap)] = send[pl.ds(hosted * cap, cap)]

    def return_rows(send, recv, n):
        def row_copy(plane, to, block):
            remote(
                send.at[pl.ds(block * cap, cap)],
                recv.at[pl.ds(hosted * cap, cap)],
                a2a_send.at[n],
                a2a_recv.at[n],
                plane,
                2 * to + core,
            ).start()

        row_copy(behind, col, n_col + col)

        @pl.loop(1, n_col)
        def _(i):
            to = lax.rem(col + i, n_col)
            row_copy(x, to, to)
            row_copy(behind, to, n_col + to)

        recv[pl.ds(hosted * cap, cap)] = send[pl.ds(col * cap, cap)]

    def wait_all(buf, sem):
        rest = buf.at[pl.ds(0, (n_ep - 1) * cap)]
        pltpu.make_async_copy(rest, rest, sem).wait()

    def tiled(src, dst):
        for j in range(tiles):
            scr[pl.ds(j, tok, stride=tiles), :] = src[:, j * LANES : (j + 1) * LANES].astype(F32)

        @pl.loop(0, tok // 8)
        def _(i):
            rows = pl.ds(pl.multiple_of(i * 8 * tiles, 16), 8 * tiles)
            dst[pl.ds(i * 8, 8)] = scr[rows, :].astype(BF16).reshape(8, tiles, LANES)

        dst[tok] = jnp.zeros((tiles, LANES), BF16)

    def row(r):
        return pl.ds(pl.multiple_of(r * tiles, 16), tiles)

    @pl.when(is_home)
    def _():
        for k in range(2):
            local_copy(k).start()

    pl.semaphore_wait(barrier, 9)

    @pl.when(is_home)
    def _():
        for k in range(2):
            for h in range(2):
                far_copy(k, h).start()
        for k in range(2):
            own_copy(k).start()

    @pl.when(not_home)
    def _():
        for k in range(2):
            for h in range(2):
                for d in range(2):
                    out_copy(k, d, h).start()

    tell(0)
    tables = [
        pltpu.make_async_copy(index_v, index_s, local_sem.at[2]),
        pltpu.make_async_copy(weight_v, weight_s, local_sem.at[3]),
    ]
    routing(ids_ref, pair_ref, index_v, weight_v, cap)
    for copy in tables:
        copy.start()
    hear(0)
    tell(1)
    tiled(tokens_ref, tok_t)
    hear(1)
    tell(2)
    for copy in tables:
        copy.wait()

    @pl.loop(0, slots // 8)
    def _(i):
        for j in range(8):
            s = i * 8 + j
            send_x[s] = tok_t[index_s[0, s]]

    hear(2)
    tell(3)
    tiled(grad_ref, grd_t)
    hear(3)
    send_rows(send_x, recv_x, 0)

    @pl.loop(0, slots // 8)
    def _(i):
        for j in range(8):
            s = i * 8 + j
            rows = grd_t[index_s[0, s]].astype(F32) * weight_s[0, s]
            send_c[s] = rows.astype(BF16)

    send_rows(send_c, recv_c, 1)

    def spread(recv, dst):
        @pl.loop(0, slots // 8)
        def _(i):
            rows = pl.ds(pl.multiple_of(i * 8 * tiles, 16), 8 * tiles)
            scr[rows, :] = recv[pl.ds(i * 8, 8)].astype(F32).reshape(8 * tiles, LANES)

        for q in range(n_rep):
            for j in range(per_q):
                dst[q, :, j * LANES : (j + 1) * LANES] = scr[
                    pl.ds(q * per_q + j, slots, stride=tiles), :
                ].astype(BF16)

    def place(s):
        return lax.rem(x + s, n_rep)

    def product(s, lhs, rhs, out, columns, step, first):
        @pl.loop(0, columns // step)
        def _(n):
            cols = pl.ds(pl.multiple_of(n * step, LANES), step)
            y = jnp.dot(lhs[place(s)], rhs[s, :, cols], preferred_element_type=F32)
            if first:
                out[:, cols] = y
            else:
                out[:, cols] = out[:, cols] + y

    def returned(lhs, rhs, send):
        for q in range(n_rep):
            s = lax.rem(q + n_rep - x, n_rep)
            for j in range(per_q):
                scr[pl.ds(q * per_q + j, slots, stride=tiles), :] = lax.dot_general(
                    lhs[...],
                    rhs[s, j * LANES : (j + 1) * LANES, :],
                    (((1,), (1,)), ((), ())),
                    preferred_element_type=F32,
                )

        @pl.loop(0, slots // 8)
        def _(i):
            rows = pl.ds(pl.multiple_of(i * 8 * tiles, 16), 8 * tiles)
            send[pl.ds(i * 8, 8)] = scr[rows, :].astype(BF16).reshape(8, tiles, LANES)

    def outer(lhs, rhs, s, rows, k, columns, step):
        block = lhs[place(s), :, rows]

        @pl.loop(0, columns // step)
        def _(n):
            cols = pl.ds(pl.multiple_of(n * step, LANES), step)
            y = lax.dot_general(
                block, rhs[:, cols], (((0,), (0,)), ((), ())), preferred_element_type=F32
            )
            part[k][s, rows, cols] = y.astype(BF16)

    def partial_grads(lhs, rhs, k, columns, step):
        for s in (2, 1, 3):
            outer(lhs, rhs, s, other_half, k, columns, step)
            swap_copy(k, s).start()
        if k == 1:
            far_arrives(1)
        for s in (2, 1, 3):
            outer(lhs, rhs, s, mine, k, columns, step)
            swap_copy(k, s).wait_recv()

            @pl.loop(0, half // 16)
            def _(i):
                here = pl.ds(pl.multiple_of(i * 16, 16), 16)
                there = pl.ds(pl.multiple_of(core * half + i * 16, 16), 16)
                total = part[k][s, there, :].astype(F32) + pin[k][s - 1, here, :].astype(F32)
                part[k][s, there, :] = total.astype(BF16)

            if s == 2:
                ret_copy(k).start()
            else:
                near_copy(k, s // 2).start()

    def home_grads(lhs, rhs, k, columns, step):
        for h in range(2):
            outer(lhs, rhs, 0, halves[h], k, columns, step)

        @pl.when(not_home)
        def _():
            home_copy(k).start()

    def pass_on(k):
        ret_copy(k).wait_recv()
        fin_copy(k).start()

    def finish(k, out):
        @pl.when(is_home)
        def _():
            home_copy(k).wait_recv()

        for h in range(2):
            arrived = [
                remote(
                    back[k], din[k].at[d, halves[h], :], fin_send.at[k], near_recv.at[k, d, h], x, mate
                )
                for d in range(2)
            ]
            arrived[0].wait_recv()

            @pl.when(is_home)
            def _():
                @pl.loop(0, half // 16)
                def _(i):
                    rows = pl.ds(pl.multiple_of(h * half + i * 16, 16), 16)
                    total = part[k][0, rows, :].astype(F32) + home[k][rows, :].astype(F32)
                    out[rows, :] = (total + din[k][0, rows, :].astype(F32)).astype(BF16)

            @pl.when(not_home)
            def _():
                arrived[1].wait_recv()

                @pl.loop(0, half // 16)
                def _(i):
                    rows = pl.ds(pl.multiple_of(h * half + i * 16, 16), 16)
                    total = din[k][0, rows, :].astype(F32) + din[k][1, rows, :].astype(F32)
                    out[rows, :] = total.astype(BF16)

    def near_arrives(k):
        for d in range(2):
            out_copy(k, d, 0).wait_recv()
            mate_copy(k, 3 - 2 * d).start()

    def far_arrives(k):
        fwd_copy(k).wait_recv()
        mate_copy(k, 2).start()

    def own_arrives(k):
        @pl.when(is_home)
        def _():
            local_copy(k).wait()

        @pl.when(not_home)
        def _():
            own_copy(k).wait_recv()

    for k in range(2):
        far_copy(k, 0).wait_recv()
        fwd_copy(k).start()
    wait_all(recv_x, a2a_recv.at[0])
    spread(recv_x, x2)
    own_arrives(0)
    product(0, x2, wg, acc, 2 * hidden, 768, True)
    near_arrives(0)
    for s in (1, 3):
        mate_copy(0, s).wait_recv()
        product(s, x2, wg, acc, 2 * hidden, 768, False)
    near_arrives(1)
    far_arrives(0)
    mate_copy(0, 2).wait_recv()
    product(2, x2, wg, acc, 2 * hidden, 768, False)

    @pl.loop(0, slots // 16)
    def _(i):
        rows = pl.ds(pl.multiple_of(i * 16, 16), 16)
        gate = acc[rows, :hidden]
        up = acc[rows, hidden:]
        hid[rows, :] = (gate * jax.nn.sigmoid(gate) * up).astype(BF16)

    wait_all(recv_c, a2a_recv.at[1])
    spread(recv_c, c2)
    partial_grads(c2, hid, 1, hidden, 768)
    own_arrives(1)
    for s in (1, 3, 2):
        mate_copy(1, s).wait_recv()
    returned(hid, wd, send_o)
    return_rows(send_o, recv_o, 2)
    for s in range(n_rep):
        product(s, c2, wd, gh, hidden, 768, s == 0)

    @pl.loop(0, slots // 16)
    def _(i):
        rows = pl.ds(pl.multiple_of(i * 16, 16), 16)
        gate = acc[rows, :hidden]
        up = acc[rows, hidden:]
        grad = gh[rows, :]
        s = jax.nn.sigmoid(gate)
        ggu[rows, :hidden] = (grad * up * (s * (1.0 + gate * (1.0 - s)))).astype(BF16)
        ggu[rows, hidden:] = (grad * gate * s).astype(BF16)

    pass_on(1)
    partial_grads(x2, ggu, 0, 2 * hidden, 768)
    returned(ggu, wg, send_r)
    return_rows(send_r, recv_r, 3)
    home_grads(c2, hid, 1, hidden, 768)
    home_grads(x2, ggu, 0, 2 * hidden, 768)

    def untiled(out):
        for j in range(tiles):
            out[:, j * LANES : (j + 1) * LANES] = scr[pl.ds(j, tok, stride=tiles), :].astype(BF16)

    wait_all(recv_o, a2a_recv.at[2])

    @pl.loop(0, tok // 4)
    def _(i):
        for j in range(4):
            t = i * 4 + j
            first = recv_o[index_s[1, t]].astype(F32)
            second = recv_o[index_s[2, t]].astype(F32)
            grad = grd_t[t].astype(F32)
            scr[row(t), :] = weight_s[1, t] * first + weight_s[2, t] * second
            rg_a[pl.ds(t, 1), :] = jnp.sum(grad * first, axis=0, keepdims=True)
            rg_b[pl.ds(t, 1), :] = jnp.sum(grad * second, axis=0, keepdims=True)

    untiled(mixed_ref)
    rg_ref[0:1, :] = jnp.sum(rg_a[...].T, axis=0, keepdims=True)
    rg_ref[1:2, :] = jnp.sum(rg_b[...].T, axis=0, keepdims=True)

    pass_on(0)
    finish(1, gdn_ref)
    wait_all(recv_r, a2a_recv.at[3])

    @pl.loop(0, tok // 4)
    def _(i):
        for j in range(4):
            t = i * 4 + j
            first = recv_r[index_s[1, t]].astype(F32)
            second = recv_r[index_s[2, t]].astype(F32)
            scr[row(t), :] = first + second

    untiled(gtok_ref)
    finish(0, ggu_ref)

    for n, buf in enumerate((send_x, send_c, send_o, send_r)):
        wait_all(buf, a2a_send.at[n])
    for k in range(2):
        fwd_copy(k).wait_send()
        ret_copy(k).wait_send()
        fin_copy(k).wait_send()
        for s in (1, 2, 3):
            mate_copy(k, s).wait_send()
            swap_copy(k, s).wait_send()
        for d in range(2):
            near_copy(k, d).wait_send()

    @pl.when(is_home)
    def _():
        for k in range(2):
            own_copy(k).wait_send()
            for h in range(2):
                far_copy(k, h).wait_send()

    @pl.when(not_home)
    def _():
        for k in range(2):
            home_copy(k).wait_send()
            for d in range(2):
                for h in range(2):
                    out_copy(k, d, h).wait_send()


def routing(ids_ref, pair_ref, index_v, weight_v, cap):
    top, tok = ids_ref.shape
    slots = index_v.shape[1]
    here = lax.broadcasted_iota(jnp.int32, (tok, tok), 0)
    there = lax.broadcasted_iota(jnp.int32, (tok, tok), 1)
    rows = [jnp.broadcast_to(ids_ref[k : k + 1, :], (tok, tok)) for k in range(top)]
    columns = [r.T for r in rows]
    slot = lax.broadcasted_iota(jnp.int32, (tok, slots), 1)
    token = lax.broadcasted_iota(jnp.int32, (tok, slots), 0)
    source = jnp.full((1, slots), tok, jnp.int32)
    weight = jnp.zeros((1, slots), F32)
    for k in range(top):
        rank = jnp.sum(
            jnp.where((columns[k] == rows[k]) & (here < there), 1, 0), axis=0, keepdims=True
        )
        for m in range(k):
            rank = rank + jnp.sum(jnp.where(columns[m] == rows[k], 1, 0), axis=0, keepdims=True)
        target = ids_ref[k : k + 1, :] * cap + rank
        pair = pair_ref[k : k + 1, :].astype(F32)
        match = jnp.broadcast_to(target, (tok, tok)).T[:, 0:1] == slot
        pairs = jnp.broadcast_to(pair, (tok, tok)).T[:, 0:1]
        source = source + jnp.sum(jnp.where(match, token - tok, 0), axis=0, keepdims=True)
        weight = weight + jnp.sum(jnp.where(match, pairs, 0.0), axis=0, keepdims=True)
        index_v[1 + k : 2 + k, 0:tok] = target
        weight_v[1 + k : 2 + k, 0:tok] = pair
    index_v[0:1, :] = source
    weight_v[0:1, :] = weight


def copy_kernel(*refs):
    n = (len(refs) - 1) // 2
    sems = refs[-1]
    copies = [pltpu.make_async_copy(refs[i], refs[n + i], sems.at[i]) for i in range(n)]
    for copy in copies:
        copy.start()
    for copy in copies:
        copy.wait()


def per_device(n_rep, n_ep, tokens, expert_ids, route_weights, w_gate_up, w_down, grad_out):
    tok, width = tokens.shape
    top = expert_ids.shape[1]
    hidden = w_down.shape[2]
    cap = 5 * tok * top // (4 * n_ep)
    slots = n_ep * cap
    quarter = width // n_rep
    half = quarter // 2
    tiles = width // LANES
    padded = -(-slots // LANES) * LANES
    vmem = pl.BlockSpec(memory_space=pltpu.VMEM)
    anywhere = pl.BlockSpec(memory_space=pl.ANY)
    V = pltpu.VMEM
    rows = V((slots, tiles, LANES), BF16)
    dma = pltpu.SemaphoreType.DMA
    shapes = (
        ((tok, width), BF16),
        ((tok, width), BF16),
        ((quarter, 2 * hidden), BF16),
        ((quarter, hidden), BF16),
        ((top, tok), F32),
    )
    made = pl.pallas_call(
        functools.partial(layer_kernel, (n_rep, n_ep, cap, tok, width, hidden)),
        out_shape=tuple(V(*shape) for shape in shapes),
        in_specs=[vmem] * 4 + [anywhere] * 2,
        out_specs=[vmem] * 5,
        scratch_shapes=[
            V(lead + (rows_, width_), BF16)
            for lead, rows_ in (
                ((n_rep,), quarter),
                ((n_rep,), quarter),
                ((n_rep - 1,), half),
                ((), quarter),
                ((), half),
                ((), half),
                ((2,), quarter),
            )
            for width_ in (2 * hidden, hidden)
        ]
        + [rows] * 8
        + [
            V((n_rep, slots, quarter), BF16),
            V((n_rep, slots, quarter), BF16),
            V((slots * tiles, LANES), F32),
            V((slots, 2 * hidden), F32),
            V((slots, hidden), F32),
            V((slots, hidden), BF16),
            V((slots, 2 * hidden), BF16),
            V((tok + 1, tiles, LANES), BF16),
            V((tok + 1, tiles, LANES), BF16),
            V((tok, LANES), F32),
            V((tok, LANES), F32),
            V((8, padded), jnp.int32),
            V((8, padded), F32),
            pltpu.SMEM((8, padded), jnp.int32),
            pltpu.SMEM((8, padded), F32),
            dma((4,)),
            dma((2,)),
            dma((2,)),
            dma((2, 2, 2)),
            dma((2, 2)),
            dma((2, 2)),
            dma((2,)),
            dma((2,)),
            dma((2,)),
            dma((2, n_rep)),
            dma((2, n_rep)),
            dma((2, n_rep)),
            dma((2, n_rep)),
            dma((2,)),
            dma((2,)),
            dma((2, 2)),
            dma((2, 2, 2)),
            dma((2,)),
            dma((2,)),
            dma((2,)),
            dma((4,)),
            dma((4,)),
            pltpu.SemaphoreType.REGULAR((4,)),
        ],
        compiler_params=pltpu.CompilerParams(
            collective_id=0, has_side_effects=True, vmem_limit_bytes=62000000
        ),
    )(expert_ids.T, route_weights.T, tokens, grad_out, w_gate_up[0], w_down[0])
    mixed, gtok, ggu, gdn, rg = pl.pallas_call(
        copy_kernel,
        out_shape=tuple(jax.ShapeDtypeStruct(*shape) for shape in shapes),
        in_specs=[vmem] * 5,
        out_specs=[anywhere] * 5,
        scratch_shapes=[dma((5,))],
        compiler_params=pltpu.CompilerParams(vmem_limit_bytes=1 << 20),
    )(*made)
    return mixed, gtok, ggu[None], gdn[None], rg.T


def solution(mesh):
    both = ("rep", "ep")
    split = P(both, None)
    weights = P("ep", "rep", None)
    return jax.shard_map(
        functools.partial(per_device, mesh.shape["rep"], mesh.shape["ep"]),
        mesh=mesh,
        in_specs=(split, split, split, weights, weights, split),
        out_specs=(split, split, weights, weights, split),
        check_vma=False,
    )
```
